32 devices in a mesh: groups: 2 (over y), rec: 4 (over z), attr: 4 (over x, core).
Axes of the slice: x: 2, y: 2, z: 4, core: 2. Of those that a mesh axis runs over, the one named last changes fastest.
Arguments:
- cells: bfloat16 [64, 49152], P(('groups', 'rec'), 'attr'), parts along dimension 0, may hold values from -1000 to 1000
- cotangent: bfloat16 [64, 49152], P(('groups', 'rec'), 'attr'), parts along dimension 0, may hold values from -6 to 6
- qkv_attr: bfloat16 [192, 576], replicated, may hold values from -8 to 8
- out_attr: bfloat16 [192, 192], replicated, may hold values from -0.4375 to 0.4375
- qkv_samp: bfloat16 [192, 576], replicated, may hold values from -8 to 8
- out_samp: bfloat16 [192, 192], replicated, may hold values from -0.4375 to 0.4375
- up_weight: bfloat16 [192, 768], replicated, may hold values from -0.4375 to 0.4375
- down_weight: bfloat16 [768, 192], replicated, may hold values from -0.21875 to 0.21875
- train_split: int32 [64], P('groups'), parts along dimension 0, may hold values from 0 to 1, as said below
Outputs:
- grad_cells: bfloat16 [64, 49152], P(('groups', 'rec'), 'attr'), parts along dimension 0
- grad_qkv_attr: float32 [384, 576], P('groups'), parts along dimension 0
- grad_out_attr: float32 [384, 192], P('groups'), parts along dimension 0
- grad_qkv_samp: float32 [384, 576], P('groups'), parts along dimension 0
- grad_out_samp: float32 [384, 192], P('groups'), parts along dimension 0
- grad_up: float32 [384, 768], P('groups'), parts along dimension 0
- grad_down: float32 [1536, 192], P('groups'), parts along dimension 0
The draws below stay inside these ranges and needn't reach their ends.
There are 2 independent parts, one for each index of `groups`. The reference program is written for one: setup_inputs(seed, part) draws one part's arguments, and reference() takes and returns one part's arrays. A program takes and returns all parts, laid end to end along the dimension named above; an argument that names none is the same for every part. Nothing has to cross between parts.
Inputs may be any that keep to these rules, and one draw needn't show every extreme that they name: `train_split`: every table window has at least one training record.
All inputs are finite; a program needn't handle non-finite values.
Results may differ from the reference program's by a relative error of at most 0.018.
The reference program's roundings to bfloat16 on the way count: a program that leaves them out, or rounds other values in their place, can miss the bound.
Values may be sent and summed in bfloat16 or wider, within the bound.
A program may use at most 64 MiB of HBM per device.

```python
import math
import jax
import jax.numpy as jnp
from jax import lax

E = 192
HEADS = 6
FF = 768
RECORDS = 32
ATTRS = 256


def qkv_draw(key):
    base_key = jax.random.fold_in(key, 0)
    matrix = jax.random.normal(base_key, (E, 3 * E), jnp.float32) / math.sqrt(E)
    return matrix


def draw_qkv_attr(key, part):
    return qkv_draw(jax.random.fold_in(key, 11)).astype(jnp.bfloat16)


def draw_qkv_samp(key, part):
    return qkv_draw(jax.random.fold_in(key, 12)).astype(jnp.bfloat16)


def draw_cells(key, part):
    keys_all = jax.random.split(jax.random.fold_in(key, 13), 3)
    cell_scale = jnp.exp(jax.random.uniform(keys_all[1], (RECORDS, ATTRS, 1), jnp.float32, 0.0, math.log(10.0)))
    feature_scale = jnp.exp(jax.random.uniform(keys_all[2], (1, 1, E), jnp.float32, 0.0, math.log(10.0)))
    base = jax.random.normal(keys_all[0], (RECORDS, ATTRS, E), jnp.float32)
    return (base * cell_scale * feature_scale).reshape(RECORDS, ATTRS * E).astype(jnp.bfloat16)


def draw_train_split(key, part):
    first_key, second_key = jax.random.split(jax.random.fold_in(key, 14))
    coins = jax.random.randint(first_key, (RECORDS,), 0, 2)
    chosen = jax.random.randint(second_key, (), 0, RECORDS)
    return jnp.where(jnp.arange(RECORDS) == chosen, 1, coins).astype(jnp.int32)


def steps_of(stream_key, extent, cuts, low, high):
    factor_of, own = 1.0, jax.random.fold_in(stream_key, 6)
    for position, shards_of in cuts:
        steps = jnp.exp(jax.random.uniform(jax.random.fold_in(own, position), (shards_of,), jnp.float32, low / len(cuts), high / len(cuts)))
        factor_of = factor_of * jnp.repeat(steps, extent[position] // shards_of).reshape([-1 if axis == position else 1 for axis in range(len(extent))])
    return factor_of


def bell_draw(own_key, dims, deviation, limit, pieces=(), dtype=jnp.bfloat16):
    level = steps_of(own_key, dims, pieces, -0.22, 0.18) if pieces else 1.0
    result = jax.random.normal(own_key, dims, jnp.float32) * deviation * level
    return jnp.minimum(jnp.maximum(result, -limit), limit).astype(dtype)


def setup_inputs(seed: int = 0, part: int = 0) -> dict:
    seeds = jax.random.split(jax.random.key(seed), 10)
    own_keys = jax.random.split(jax.random.fold_in(seeds[9], part), 10)
    cells = draw_cells(jax.random.fold_in(jax.random.fold_in(seeds[9], part), 71), part)
    cotangent = bell_draw(own_keys[1], (RECORDS, ATTRS * E), 1.0, 6.0, ((0, 4), (1, 4)))
    qkv_attr = draw_qkv_attr(jax.random.fold_in(seeds[9], 71), part)
    out_attr = bell_draw(seeds[3], (E, E), E ** -0.5, 0.4375)
    qkv_samp = draw_qkv_samp(jax.random.fold_in(seeds[9], 71), part)
    out_samp = bell_draw(seeds[5], (E, E), E ** -0.5, 0.4375)
    up_weight = bell_draw(seeds[6], (E, FF), E ** -0.5, 0.4375)
    down_weight = bell_draw(seeds[7], (FF, E), FF ** -0.5, 0.21875)
    train_split = draw_train_split(jax.random.fold_in(jax.random.fold_in(seeds[9], part), 71), part)
    return {"cells": cells, "cotangent": cotangent, "qkv_attr": qkv_attr, "out_attr": out_attr, "qkv_samp": qkv_samp, "out_samp": out_samp, "up_weight": up_weight, "down_weight": down_weight, "train_split": train_split}


def product(form, left, right):
    return jnp.einsum(form, left.astype(jnp.float32), right.astype(jnp.float32))

def layer_norm(values):
    center = values - lax.optimization_barrier(jnp.mean(values, axis=-1, keepdims=True))
    spread = lax.optimization_barrier(jnp.mean(center * center, axis=-1, keepdims=True))
    return center * lax.rsqrt(spread + 1e-05)

def attend(cells_in, qkv_weight, out_weight, allowed):
    groups, length, width = cells_in.shape
    head_dim = width // HEADS
    as_float = cells_in.astype(jnp.float32)
    normed = layer_norm(as_float).astype(jnp.bfloat16)
    project = product('gle,ef->glf', normed, qkv_weight).astype(jnp.bfloat16)
    project = project.reshape(groups, length, 3, HEADS, head_dim)
    scores = product('gqhd,gkhd->ghqk', project[:, :, 0], project[:, :, 1]) * (1.0 / math.sqrt(head_dim))
    if allowed is not None:
        scores = jnp.where(allowed[None, None, None, :] > 0, scores, -1e+30)
    top_score = lax.stop_gradient(lax.optimization_barrier(jnp.max(scores, axis=-1, keepdims=True)))
    expo = jnp.exp(scores - top_score)
    probs = (expo / lax.optimization_barrier(jnp.sum(expo, axis=-1, keepdims=True))).astype(jnp.bfloat16)
    mixed = product('ghqk,gkhd->gqhd', probs, project[:, :, 2]).astype(jnp.bfloat16)
    mixed = mixed.reshape(groups, length, width)
    return (as_float + product('gle,ef->glf', mixed, out_weight)).astype(jnp.bfloat16)

def feed_forward(block, up_weight, down_weight):
    flat = block.reshape(-1, E)
    as_float = flat.astype(jnp.float32)
    normed = layer_norm(as_float).astype(jnp.bfloat16)
    hidden = jax.nn.gelu(product('re,ef->rf', normed, up_weight), approximate=False).astype(jnp.bfloat16)
    return (as_float + product('rf,fe->re', hidden, down_weight)).astype(jnp.bfloat16).reshape(block.shape)

def reference(cells, cotangent, qkv_attr, out_attr, qkv_samp, out_samp, up_weight, down_weight, train_split):
    rec_block = math.gcd(RECORDS, 8)
    attr_block = math.gcd(ATTRS, 8)

    def forward(table_flat, qa_weight, oa_weight, qs_weight, os_weight, first_weight, second_weight):
        table = table_flat.reshape(RECORDS // rec_block, rec_block, ATTRS, E)

        def attr_step(piece):
            return attend(piece, qa_weight, oa_weight, None)
        first = lax.map(jax.checkpoint(attr_step), table).reshape(RECORDS, ATTRS, E)
        turned = jnp.swapaxes(first, 0, 1).reshape(ATTRS // attr_block, attr_block, RECORDS, E)

        def samp_step(piece):
            return attend(piece, qs_weight, os_weight, train_split)
        second = lax.map(jax.checkpoint(samp_step), turned).reshape(ATTRS, RECORDS, E)
        second = jnp.swapaxes(second, 0, 1)
        return feed_forward(second, first_weight, second_weight).reshape(RECORDS, ATTRS * E)
    weights = (qkv_attr, out_attr, qkv_samp, out_samp, up_weight, down_weight)
    weights = tuple((matrix.astype(jnp.float32) for matrix in weights))
    output_cells, puller = jax.vjp(forward, cells, *weights)
    grads = puller(cotangent)
    factor = 1.0 / math.sqrt(RECORDS * ATTRS)
    return (grads[0], grads[1] * factor, grads[2] * factor, grads[3] * factor, grads[4] * factor, grads[5] * factor, grads[6] * factor)
```

```python
import functools
import math

import jax
import jax.numpy as jnp
import numpy as np
from jax import lax
from jax.experimental import pallas as pl
from jax.experimental.pallas import tpu as pltpu
from jax.sharding import PartitionSpec as P

E = 192
HEADS = 6
HD = E // HEADS
SCALE = 1.0 / math.sqrt(HD)
BLOCKS = 16
F32 = jnp.float32
BF16 = jnp.bfloat16
MESH = pl.DeviceIdType.MESH
NN = (((1,), (0,)), ((), ()))
NT = (((1,), (1,)), ((), ()))
TN = (((0,), (0,)), ((), ()))
VMEM = pl.BlockSpec(memory_space=pltpu.VMEM)
ANY = pl.BlockSpec(memory_space=pl.ANY)
HBM = pl.BlockSpec(memory_space=pltpu.HBM)


def dot(a, b, form=NN):
    return lax.dot_general(a, b, form, preferred_element_type=F32)


def place(sizes, order):
    index = np.arange(math.prod(sizes)).reshape(sizes).transpose(order).reshape(-1)
    there = np.empty_like(index)
    there[index] = np.arange(index.size)
    return there.astype(np.int32)


def moved(where_ref, x):
    n = x.shape[0]
    hot = lax.broadcasted_iota(jnp.int32, (n, n), 0) == where_ref[...]
    return dot(jnp.where(hot, 1.0, 0.0).astype(BF16), x)


def put(ref, b, value):
    pieces, part = ref.shape[1], ref.shape[2]
    side = jnp.concatenate([value[: E // 2], value[E // 2:]], axis=1)
    for r in range(pieces):
        ref[b, r] = side[r * part:(r + 1) * part].astype(BF16)


def pack(ref, value, few):
    run = value.shape[0] // few
    pieces, part = ref.shape[0], ref.shape[1]
    side = jnp.concatenate([value[k * run:(k + 1) * run] for k in range(few)], axis=1)
    for r in range(pieces):
        ref[r] = side[r * part:(r + 1) * part].astype(BF16)


def unpack(ref, flat, few):
    pieces, part = ref.shape[0], ref.shape[1]
    run = pieces * part
    for r in range(pieces):
        side = ref[r].astype(F32)
        for k in range(few):
            flat[k * run + r * part:k * run + (r + 1) * part] = side[:, k * E:(k + 1) * E]
    return flat[...].astype(BF16)


def norm(x):
    center = x - jnp.mean(x, axis=-1, keepdims=True)
    scale = lax.rsqrt(jnp.mean(center * center, axis=-1, keepdims=True) + 1e-05)
    return center * scale, scale


def norm_back(hat, scale, grad):
    return scale * (
        grad
        - jnp.mean(grad, axis=-1, keepdims=True)
        - hat * jnp.mean(grad * hat, axis=-1, keepdims=True)
    )


def attend(x_ref, qkv, out, qkv_s, p_s, acc, n, size, bias):
    normed = norm(x_ref[...].astype(F32))[0].astype(BF16)
    for t in range(3):
        qkv_s[t] = dot(normed, qkv[:, t * E:(t + 1) * E]).T.astype(BF16)

    def head(h):
        rows = pl.ds(h * HD, HD)
        for b in range(n):
            cols = pl.ds(b * size, size)
            s = dot(qkv_s[1, rows, cols], qkv_s[0, rows, cols], TN) * SCALE
            if bias is not None:
                s = jnp.where(bias[...] > 0, s, -1e30)
            e = jnp.exp(s - jnp.max(s, axis=0, keepdims=True))
            p = e * (1.0 / jnp.sum(e, axis=0, keepdims=True))
            p_s[b, h] = p
            acc[0, rows, cols] = dot(qkv_s[2, rows, cols], p.astype(BF16))

    for h in range(HEADS):
        head(h)
    mixed = acc[0].T.astype(BF16)
    return normed, mixed, (x_ref[...].astype(F32) + dot(mixed, out)).astype(BF16)


def heads_back(g, out, qkv_s, p_s, acc, dm_s, n, size, between):
    dm_s[...] = dot(out, g, NT).astype(BF16)

    def head(h):
        rows = pl.ds(h * HD, HD)
        for b in range(n):
            cols = pl.ds(b * size, size)
            dm = dm_s[rows, cols]
            p = p_s[b, h]
            dp = dot(qkv_s[2, rows, cols], dm, TN).astype(BF16).astype(F32)
            ds = (p * (dp - jnp.sum(dp * p, axis=0, keepdims=True)) * SCALE).astype(BF16)
            acc[0, rows, cols] = dot(qkv_s[1, rows, cols], ds)
            acc[1, rows, cols] = dot(qkv_s[0, rows, cols], ds, NT)
            acc[2, rows, cols] = dot(dm, p.astype(BF16), NT)

    for h in range(HEADS):
        head(h)
        between.get(h, lambda: None)()


def weights_back(normed, d_s, grads, first):
    for t in range(3):
        put(grads, first + t, dot(normed, d_s[t], TN))


def input_back(hat, scale, g, d_s, qkv):
    dn = None
    for t in range(3):
        part = dot(d_s[t], qkv[:, t * E:(t + 1) * E], NT)
        dn = part if dn is None else dn + part
    return (g.astype(F32) + norm_back(hat, scale, dn.astype(BF16).astype(F32))).astype(BF16)


def rows_of(cells, flat):
    rows = cells.shape[0]
    for a in range(cells.shape[1] // E):
        flat[a * rows:(a + 1) * rows] = cells[:, a * E:(a + 1) * E].astype(F32)
    return flat[...].astype(BF16)


def shifts_of(axes):
    sizes = [lax.axis_size(a) for a in axes]
    return [s for s in np.ndindex(*sizes) if any(s)], sizes


def peers_of(axes):
    shifts, sizes = shifts_of(axes)
    me = [lax.axis_index(a) for a in axes]
    return [[lax.rem(m + d, n) for m, d, n in zip(me, s, sizes)] for s in shifts]


def start_swap(axes, src, dst, sems):
    _, sizes = shifts_of(axes)

    def flat(where):
        number = where[0]
        for w, n in zip(where[1:], sizes[1:]):
            number = number * n + w
        return number

    me = flat([lax.axis_index(a) for a in axes])
    copies = []
    for k, to in enumerate(peers_of(axes)):
        copy = pltpu.make_async_remote_copy(
            src_ref=src.at[flat(to)],
            dst_ref=dst.at[me],
            send_sem=sems.at[0, k],
            recv_sem=sems.at[1, k],
            device_id=dict(zip(axes, to)),
            device_id_type=MESH,
        )
        copy.start()
        copies.append(copy)
    dst[me] = src[me]
    return copies


def settle(copies):
    for copy in copies:
        copy.wait()


def total_steps(buf, out, first, count, r1, r2, s1, sems):
    rec, attr = lax.axis_index("rec"), lax.axis_index("attr")
    n_rec, n_x = lax.axis_size("rec"), lax.axis_size("attr") // 2
    half, x = lax.rem(attr, 2), lax.div(attr, 2)
    h1 = count // 2
    h2 = h1 // n_x
    base = first + half * h1 + x * h2
    sem = iter(range(sems.shape[1]))

    def push(src, dst, device):
        k = next(sem)
        copy = pltpu.make_async_remote_copy(
            src_ref=src, dst_ref=dst, send_sem=sems.at[0, k], recv_sem=sems.at[1, k],
            device_id=device, device_id_type=MESH,
        )
        copy.start()
        return copy

    partner = {"attr": x * 2 + 1 - half}
    chips = [
        (lax.rem(rec + d, n_rec), lax.rem(x + c, n_x)) for d, c in np.ndindex(n_rec, n_x) if d or c
    ]
    copies = [push(buf.at[pl.ds(first + (1 - half) * h1, h1)], r1, partner)]
    yield
    settle(copies)
    for b in range(h1):
        s1[b] = (buf[first + half * h1 + b].astype(F32) + r1[b].astype(F32)).astype(BF16)
    copies = [
        push(s1.at[pl.ds(c * h2, h2), r], r2.at[k], {"rec": r, "attr": c * 2 + half})
        for k, (r, c) in enumerate(chips)
    ]
    yield
    settle(copies)
    for b in range(h2):
        value = s1[x * h2 + b, rec].astype(F32)
        for k in range(len(chips)):
            value += r2[k, b].astype(F32)
        out[base + b, rec] = value.astype(BF16)
    own = out.at[pl.ds(base, h2), rec]
    copies = [push(own, own, {"rec": r, "attr": c * 2 + half}) for r, c in chips]
    yield
    settle(copies)
    own = out.at[pl.ds(first + half * h1, h1)]
    copies = [push(own, own, partner)]
    yield
    settle(copies)
    yield


COUNTS = (4, 4, 4, 4)
UP = (0, 1, 4, 5)
DOWN = (2, 3, 6, 7)


def layer_kernel(
    size_a, size_s, length, few,
    cells_h, cot_h, qkva_h, outa_h, qkvs_h, outs_h, up_h, down_h, split_h, place_h,
    o_got, totals,
    cells, cot, qkva, outa, qkvs, outs, up, down, split, places, in_sems,
    flat, c_send, c_got, g_send, g_got, f_send, f_got, b_send, b_got, o_send,
    x_a, mixed_a, qkv_a, p_a, x_s, g_s, qkv_s, p_s, acc, d_s, dm_s, dn_s, bias, grads,
    c_sems, g_sems, f_sems, b_sems, o_sems, *sums,
):
    tokens = flat.shape[0]
    n_a, n_s = tokens // size_a, tokens // size_s
    loads = {}
    pairs = (
        (cells_h, cells), (place_h, places), (cot_h, cot), (qkva_h, qkva), (outa_h, outa),
        (split_h, split), (qkvs_h, qkvs), (outs_h, outs), (up_h, up), (down_h, down),
    )
    for k, (src, dst) in enumerate(pairs):
        loads[k] = pltpu.make_async_copy(src, dst, in_sems.at[k])
        loads[k].start()
    barrier = pltpu.get_barrier_semaphore()
    peers = peers_of(("rec", "attr"))
    for r, a in peers:
        pl.semaphore_signal(barrier, inc=1, device_id={"rec": r, "attr": a}, device_id_type=MESH)

    def at(k):
        return places.at[k:k + 1]

    loads[0].wait()
    loads[1].wait()
    pack(c_send, moved(at(0), rows_of(cells, flat)), few)
    pl.semaphore_wait(barrier, len(peers))
    c_copies = start_swap(("attr",), c_send, c_got, c_sems)
    loads[2].wait()
    pack(g_send, moved(at(1), rows_of(cot, flat)), few)
    g_copies = start_swap(("rec",), g_send, g_got, g_sems)
    for k in range(3, len(pairs)):
        loads[k].wait()
    settle(c_copies)
    x_a[...] = unpack(c_got, flat, few)
    _, mixed, first = attend(x_a, qkva, outa[...], qkv_a, p_a, acc, n_a, size_a, None)
    mixed_a[...] = mixed
    pack(f_send, moved(at(2), first), few)
    f_copies = start_swap(("rec", "attr"), f_send, f_got, f_sems)

    row = lax.broadcasted_iota(jnp.int32, (size_s, size_s), 0)
    column = lax.broadcasted_iota(jnp.int32, (size_s, size_s), 1)
    same = None
    for s in range(size_s // length):
        low, high = s * length, (s + 1) * length
        inside = (row >= low) & (row < high) & (column >= low) & (column < high)
        same = inside if same is None else same | inside
    tiled = jnp.concatenate([split[...].astype(F32)] * (size_s // length), axis=1)
    bias[...] = jnp.where(same, tiled, 0.0).T
    settle(g_copies)
    g_s[...] = moved(at(4), unpack(g_got, flat, few)).astype(BF16)
    settle(f_copies)
    x_s[...] = moved(at(3), unpack(f_got, flat, few)).astype(BF16)
    _, mixed, second = attend(x_s, qkvs, outs[...], qkv_s, p_s, acc, n_s, size_s, bias)
    starts = [sum(COUNTS[:k]) for k in range(4)]
    ffn1, ffn2, samp, attr = (
        total_steps(grads, totals, starts[k], COUNTS[k], *sums[4 * k:4 * k + 4]) for k in range(4)
    )
    hat, scale = norm(second.astype(F32))
    normed = hat.astype(BF16)
    g = g_s[...]
    for c in range(up.shape[1] // E):
        w_up = up[:, c * E:(c + 1) * E]
        pre = dot(normed, w_up)
        cdf = 0.5 * (1.0 + lax.erf(pre * (1.0 / math.sqrt(2.0))))
        hidden = (pre * cdf).astype(BF16)
        slope = cdf + pre * (jnp.exp(pre * pre * -0.5) * (1.0 / math.sqrt(2.0 * math.pi)))
        dh = dot(g, down[:, c * E:(c + 1) * E]).astype(BF16).astype(F32)
        dpre = (dh * slope).astype(BF16)
        put(grads, UP[c], dot(normed, dpre, TN))
        put(grads, DOWN[c], dot(g, hidden, TN))
        part = dot(dpre, w_up, NT)
        if c == 0:
            dn_s[...] = part
        else:
            dn_s[...] += part
        if c == 1:
            next(ffn1)
    next(ffn2)
    next(ffn1)
    dn = dn_s[...].astype(BF16).astype(F32)
    g = (g.astype(F32) + norm_back(hat, scale, dn)).astype(BF16)

    def go(*groups):
        def step():
            for group in groups:
                next(group)
        return step

    heads_back(
        g, outs[...], qkv_s, p_s, acc, dm_s, n_s, size_s, {1: go(ffn2)},
    )
    hat, scale = norm(x_s[...].astype(F32))
    for t in range(3):
        d_s[t] = acc[t].T.astype(BF16)
    back = input_back(hat, scale, g, d_s, qkvs)
    pack(b_send, moved(at(5), back), few)
    b_copies = start_swap(("rec", "attr"), b_send, b_got, b_sems)
    next(ffn1)
    put(grads, starts[2] + 3, dot(mixed, g, TN))
    weights_back(hat.astype(BF16), d_s, grads, starts[2])
    go(samp, samp, ffn2)()
    settle(b_copies)
    g = moved(at(6), unpack(b_got, flat, few)).astype(BF16)
    put(grads, starts[3] + 3, dot(mixed_a[...], g, TN))
    heads_back(
        g, outa[...], qkv_a, p_a, acc, dm_s, n_a, size_a, {2: go(ffn1), 4: go(samp), 5: go(ffn2)},
    )
    hat, scale = norm(x_a[...].astype(F32))
    for t in range(3):
        d_s[t] = acc[t].T.astype(BF16)
    weights_back(hat.astype(BF16), d_s, grads, starts[3])
    next(attr)
    back = input_back(hat, scale, g, d_s, qkva)
    pack(o_send, back.astype(F32), few)
    o_copies = start_swap(("attr",), o_send, o_got, o_sems)
    for steps in (attr, ffn1, ffn2, samp, attr, samp, attr, attr):
        next(steps)
    settle(o_copies)


def finish_kernel(
    factor, few, tokens_h, places_h, total_h, cells, qa, oa, qs, os, gu, gd,
    tokens, places, total, sems, flat, out_flat, tmp,
):
    loads = [
        pltpu.make_async_copy(src, dst, sems.at[k])
        for k, (src, dst) in enumerate(((tokens_h, tokens), (places_h, places), (total_h, total)))
    ]
    for load in loads:
        load.start()
    rows = cells.shape[0]
    loads[0].wait()
    loads[1].wait()
    out_flat[...] = moved(places.at[7:8], unpack(tokens, flat, few))
    for a in range(0, cells.shape[1] // E, 2):
        pair = [out_flat[(a + k) * rows:(a + k + 1) * rows] for k in range(2)]
        cells[:, a * E:(a + 2) * E] = jnp.concatenate(pair, axis=1).astype(BF16)
    loads[2].wait()

    def block(b):
        part = total.shape[2]
        for r in range(total.shape[1]):
            tmp[b, r * part:(r + 1) * part] = total[b, r].astype(F32) * factor
        side = tmp[b]
        return jnp.concatenate([side[:, :E], side[:, E:]], axis=0)

    gu[...] = jnp.concatenate([block(c) for c in UP], axis=1)
    gd[...] = jnp.concatenate([block(c) for c in DOWN], axis=1)
    for ref, start in ((qs, 8), (qa, 12)):
        ref[...] = jnp.concatenate([block(start + t) for t in range(3)], axis=1)
    os[...] = block(11)
    oa[...] = block(15)


def local(
    cells, cotangent, qkv_attr, out_attr, qkv_samp, out_samp, up_weight, down_weight, train_split
):
    n_rec, n_attr = lax.axis_size("rec"), lax.axis_size("attr")
    rows, cols = cells.shape[0], cells.shape[1] // E
    tokens = rows * cols
    width = cols * n_attr
    length = rows * n_rec
    few = rows // n_attr
    thin = cols // n_rec
    size = length * max(1, min(256 // length, thin))
    places = jnp.asarray(np.stack([
        place((cols, n_attr, few), (2, 1, 0)),
        place((n_rec, thin, n_attr, few), (3, 0, 1, 2)),
        place((few, n_attr, n_rec, thin), (0, 2, 1, 3)),
        place((few, n_rec, n_attr, thin), (3, 1, 2, 0)),
        place((few, n_rec, thin, n_attr), (2, 1, 3, 0)),
        place((thin, n_rec, n_attr, few), (3, 1, 2, 0)),
        place((few, n_rec, n_attr, thin), (0, 2, 1, 3)),
        place((few, n_attr, cols), (2, 1, 0)),
    ]))
    split = train_split[None, :]
    all_devices = n_rec * n_attr
    part = E // 2 // n_rec
    n_x = n_attr // 2

    def shape(*dims, dtype=BF16):
        return jax.ShapeDtypeStruct(dims, dtype)

    def vmem(*dims, dtype=BF16):
        return pltpu.VMEM(dims, dtype)

    args = (
        cells, cotangent, qkv_attr, out_attr, qkv_samp, out_samp, up_weight, down_weight.T, split, places
    )
    c_buf = vmem(n_attr, cols, few * E)
    g_buf = vmem(n_rec, thin * n_attr, few * E)
    f_buf = vmem(all_devices, thin, few * E)
    table = vmem(tokens, E)
    sums = []
    for count in COUNTS:
        h1 = count // 2
        h2 = h1 // n_x
        sums += [
            vmem(h1, n_rec, part, 2 * E), vmem(n_rec * n_x - 1, h2, part, 2 * E),
            vmem(h1, n_rec, part, 2 * E), pltpu.SemaphoreType.DMA((2, 2 * n_rec * n_x)),
        ]
    o_got, totals = pl.pallas_call(
        functools.partial(layer_kernel, width, size, length, few),
        out_shape=[shape(n_attr, cols, few * E), shape(BLOCKS, n_rec, part, 2 * E)],
        in_specs=[HBM] * len(args),
        out_specs=[VMEM] * 2,
        scratch_shapes=[pltpu.VMEM(a.shape, a.dtype) for a in args]
        + [
            pltpu.SemaphoreType.DMA((len(args),)),
            vmem(tokens, E, dtype=F32), c_buf, c_buf, g_buf, g_buf, f_buf, f_buf, f_buf, f_buf, c_buf,
            table, table, vmem(3, E, tokens), vmem(tokens // width, HEADS, width, width, dtype=F32),
            table, table, vmem(3, E, tokens), vmem(tokens // size, HEADS, size, size, dtype=F32),
            vmem(3, E, tokens, dtype=F32), vmem(3, tokens, E), vmem(E, tokens), vmem(tokens, E, dtype=F32),
            vmem(size, size, dtype=F32), vmem(BLOCKS, n_rec, part, 2 * E),
        ]
        + [
            pltpu.SemaphoreType.DMA((2, n))
            for n in (n_attr, n_rec, all_devices, all_devices, n_attr)
        ]
        + sums,
        compiler_params=pltpu.CompilerParams(
            collective_id=0, has_side_effects=True, vmem_limit_bytes=67043328
        ),
    )(*args)
    outs = [
        shape(rows, cols * E), shape(E, 3 * E, dtype=F32), shape(E, E, dtype=F32),
        shape(E, 3 * E, dtype=F32), shape(E, E, dtype=F32),
        shape(E, 4 * E, dtype=F32), shape(E, 4 * E, dtype=F32),
    ]
    last = (o_got, places, totals)
    out = pl.pallas_call(
        functools.partial(finish_kernel, 1.0 / math.sqrt(length * width), few),
        out_shape=outs,
        in_specs=[ANY] * 3,
        out_specs=[VMEM] * len(outs),
        scratch_shapes=[pltpu.VMEM(a.shape, a.dtype) for a in last]
        + [
            pltpu.SemaphoreType.DMA((3,)), vmem(tokens, E, dtype=F32), vmem(tokens, E, dtype=F32),
            vmem(BLOCKS, E // 2, 2 * E, dtype=F32),
        ],
        compiler_params=pltpu.CompilerParams(vmem_limit_bytes=67043328),
    )(*last)
    return (*out[:6], out[6].T)


def solution(mesh):
    both = P(("groups", "rec"), "attr")
    in_specs = (both, both, P(), P(), P(), P(), P(), P(), P("groups"))
    out_specs = (both,) + (P("groups", None),) * 6
    return jax.shard_map(local, mesh=mesh, in_specs=in_specs, out_specs=out_specs, check_vma=False)
```

```python
import functools
import math

import jax
import jax.numpy as jnp
import numpy as np
from jax import lax
from jax.experimental import pallas as pl
from jax.experimental.pallas import tpu as pltpu
from jax.sharding import PartitionSpec as P

E = 192
HEADS = 6
HD = E // HEADS
SCALE = 1.0 / math.sqrt(HD)
BLOCKS = 16
F32 = jnp.float32
BF16 = jnp.bfloat16
MESH = pl.DeviceIdType.MESH
NN = (((1,), (0,)), ((), ()))
NT = (((1,), (1,)), ((), ()))
TN = (((0,), (0,)), ((), ()))
VMEM = pl.BlockSpec(memory_space=pltpu.VMEM)
ANY = pl.BlockSpec(memory_space=pl.ANY)
HBM = pl.BlockSpec(memory_space=pltpu.HBM)


def dot(a, b, form=NN):
    return lax.dot_general(a, b, form, preferred_element_type=F32)


def place(sizes, order):
    index = np.arange(math.prod(sizes)).reshape(sizes).transpose(order).reshape(-1)
    there = np.empty_like(index)
    there[index] = np.arange(index.size)
    return there.astype(np.int32)


def mover(where_ref):
    n = where_ref.shape[1]
    hot = lax.broadcasted_iota(jnp.int32, (n, n), 0) == where_ref[...]
    return jnp.where(hot, 1.0, 0.0).astype(BF16)


def moved(where_ref, x):
    return dot(mover(where_ref), x)


def put(ref, b, value):
    pieces, part = ref.shape[1], ref.shape[2]
    side = jnp.concatenate([value[: E // 2], value[E // 2:]], axis=1)
    for r in range(pieces):
        ref[b, r] = side[r * part:(r + 1) * part].astype(BF16)


def pack(ref, value, few):
    run = value.shape[0] // few
    pieces, part = ref.shape[0], ref.shape[1]
    side = jnp.concatenate([value[k * run:(k + 1) * run] for k in range(few)], axis=1)
    for r in range(pieces):
        ref[r] = side[r * part:(r + 1) * part].astype(BF16)


def unpack(ref, flat, few):
    pieces, part = ref.shape[0], ref.shape[1]
    run = pieces * part
    for r in range(pieces):
        side = ref[r].astype(F32)
        for k in range(few):
            flat[k * run + r * part:k * run + (r + 1) * part] = side[:, k * E:(k + 1) * E]
    return flat[...].astype(BF16)


def norm(x):
    center = x - jnp.mean(x, axis=-1, keepdims=True)
    scale = lax.rsqrt(jnp.mean(center * center, axis=-1, keepdims=True) + 1e-05)
    return center * scale, scale


def norm_back(hat, scale, grad):
    return scale * (
        grad
        - jnp.mean(grad, axis=-1, keepdims=True)
        - hat * jnp.mean(grad * hat, axis=-1, keepdims=True)
    )


def attend(x_ref, qkv, out, qkv_s, p_s, acc, n, size, bias, kept):
    hat, scale = norm(x_ref[...].astype(F32))
    normed = hat.astype(BF16)
    if kept is not None:
        kept[0][...], kept[1][...] = hat, scale
    for t in range(3):
        qkv_s[t] = dot(normed, qkv[:, t * E:(t + 1) * E]).T.astype(BF16)

    def head(h):
        rows = pl.ds(h * HD, HD)
        for b in range(n):
            cols = pl.ds(b * size, size)
            s = dot(qkv_s[1, rows, cols], qkv_s[0, rows, cols], TN) * SCALE
            if bias is not None:
                s = jnp.where(bias[...] > 0, s, -1e30)
            e = jnp.exp(s - jnp.max(s, axis=0, keepdims=True))
            p = e * (1.0 / jnp.sum(e, axis=0, keepdims=True))
            p_s[b, h] = p
            acc[0, rows, cols] = dot(qkv_s[2, rows, cols], p.astype(BF16))

    for h in range(HEADS):
        head(h)
    mixed = acc[0].T.astype(BF16)
    return normed, mixed, (x_ref[...].astype(F32) + dot(mixed, out)).astype(BF16)


def heads_back(g, out, qkv_s, p_s, acc, dm_s, n, size, between):
    dm_s[...] = dot(out, g, NT).astype(BF16)

    def head(h):
        rows = pl.ds(h * HD, HD)
        for b in range(n):
            cols = pl.ds(b * size, size)
            dm = dm_s[rows, cols]
            p = p_s[b, h]
            dp = dot(qkv_s[2, rows, cols], dm, TN).astype(BF16).astype(F32)
            ds = (p * (dp - jnp.sum(dp * p, axis=0, keepdims=True)) * SCALE).astype(BF16)
            acc[0, rows, cols] = dot(qkv_s[1, rows, cols], ds)
            acc[1, rows, cols] = dot(qkv_s[0, rows, cols], ds, NT)
            acc[2, rows, cols] = dot(dm, p.astype(BF16), NT)

    for h in range(HEADS):
        head(h)
        between.get(h, lambda: None)()


def weights_back(normed, d_s, grads, first):
    for t in range(3):
        put(grads, first + t, dot(normed, d_s[t], TN))


def input_back(hat, scale, g, d_s, qkv):
    dn = None
    for t in range(3):
        part = dot(d_s[t], qkv[:, t * E:(t + 1) * E], NT)
        dn = part if dn is None else dn + part
    return (g.astype(F32) + norm_back(hat, scale, dn.astype(BF16).astype(F32))).astype(BF16)


def rows_of(cells, flat):
    rows = cells.shape[0]
    for a in range(cells.shape[1] // E):
        flat[a * rows:(a + 1) * rows] = cells[:, a * E:(a + 1) * E].astype(F32)
    return flat[...].astype(BF16)


def shifts_of(axes):
    sizes = [lax.axis_size(a) for a in axes]
    return [s for s in np.ndindex(*sizes) if any(s)], sizes


def peers_of(axes):
    shifts, sizes = shifts_of(axes)
    me = [lax.axis_index(a) for a in axes]
    return [[lax.rem(m + d, n) for m, d, n in zip(me, s, sizes)] for s in shifts]


def start_swap(axes, src, dst, sems):
    _, sizes = shifts_of(axes)

    def flat(where):
        number = where[0]
        for w, n in zip(where[1:], sizes[1:]):
            number = number * n + w
        return number

    me = flat([lax.axis_index(a) for a in axes])
    copies = []
    for k, to in enumerate(peers_of(axes)):
        copy = pltpu.make_async_remote_copy(
            src_ref=src.at[flat(to)],
            dst_ref=dst.at[me],
            send_sem=sems.at[0, k],
            recv_sem=sems.at[1, k],
            device_id=dict(zip(axes, to)),
            device_id_type=MESH,
        )
        copy.start()
        copies.append(copy)
    dst[me] = src[me]
    return copies


def settle(copies):
    for copy in copies:
        copy.wait()


def total_steps(wide, saves, kept, save_sem, buf, out, first, count, r1, r2, s1, sems):
    rec, attr = lax.axis_index("rec"), lax.axis_index("attr")
    n_rec, n_x = lax.axis_size("rec"), lax.axis_size("attr") // 2
    half, x = lax.rem(attr, 2), lax.div(attr, 2)
    h1 = count // 2
    h2 = h1 // n_x
    base = first + half * h1 + x * h2
    sem = iter(range(sems.shape[1]))

    def push(src, dst, device):
        k = next(sem)
        copy = pltpu.make_async_remote_copy(
            src_ref=src, dst_ref=dst, send_sem=sems.at[0, k], recv_sem=sems.at[1, k],
            device_id=device, device_id_type=MESH,
        )
        copy.start()
        return copy

    partner = {"attr": x * 2 + 1 - half}
    chips = [
        (lax.rem(rec + d, n_rec), lax.rem(x + c, n_x)) for d, c in np.ndindex(n_rec, n_x) if d or c
    ]
    copies = [push(buf.at[pl.ds(first + (1 - half) * h1, h1)], r1, partner)]
    yield
    settle(copies)
    for b in range(h1):
        s1[b] = (buf[first + half * h1 + b].astype(F32) + r1[b].astype(F32)).astype(BF16)
    copies = [
        push(s1.at[pl.ds(c * h2, h2), r], r2.at[k], {"rec": r, "attr": c * 2 + half})
        for k, (r, c) in enumerate(chips)
    ]
    yield
    settle(copies)
    for b in range(h2):
        value = s1[x * h2 + b, rec].astype(F32)
        for k in range(len(chips)):
            value += r2[k, b].astype(F32)
        out[base + b, rec] = value.astype(BF16)
    own = out.at[pl.ds(base, h2), rec]
    if wide:
        copies = [push(own, own, {"rec": r, "attr": c * 2 + half}) for r, c in chips]
    else:
        copies = [push(own, own, {"rec": lax.rem(rec + d, n_rec)}) for d in range(1, n_rec)]
        yield
        settle(copies)
        own = out.at[pl.ds(base, h2)]
        copies = [push(own, own, {"attr": lax.rem(x + c, n_x) * 2 + half}) for c in range(1, n_x)]
    yield
    settle(copies)
    own = out.at[pl.ds(first + half * h1, h1)]
    copies = [push(own, own, partner)]
    yield
    settle(copies)
    group = pl.ds(first, count)
    save = pltpu.make_async_copy(out.at[group], kept.at[group], save_sem)
    save.start()
    saves.append(save)
    yield


COUNTS = (4, 4, 4, 4)
KEPT = (2, 3, 5, 6)
UP = (0, 1, 4, 5)
DOWN = (2, 3, 6, 7)


def layer_kernel(
    size_a, size_s, length, few,
    cells_h, cot_h, qkva_h, outa_h, qkvs_h, outs_h, up_h, down_h, split_h, place_h,
    o_h, totals_h,
    o_got, totals, save_sems, cells, cot, qkva, outa, qkvs, outs, up, down, split, places, in_sems,
    flat, c_send, c_got, g_send, g_got, f_send, f_got, b_send, b_got, o_send,
    x_a, mixed_a, qkv_a, p_a, x_s, g_s, qkv_s, p_s, acc, d_s, dm_s, dn_s, hat_s, scale_s, hots, bias, grads,
    c_sems, g_sems, f_sems, b_sems, o_sems, *sums,
):
    tokens = flat.shape[0]
    n_a, n_s = tokens // size_a, tokens // size_s
    loads = {}
    pairs = (
        (cells_h, cells), (place_h, places), (cot_h, cot), (qkva_h, qkva), (outa_h, outa),
        (split_h, split), (qkvs_h, qkvs), (outs_h, outs), (up_h, up), (down_h, down),
    )
    for k, (src, dst) in enumerate(pairs):
        loads[k] = pltpu.make_async_copy(src, dst, in_sems.at[k])
        loads[k].start()
    barrier = pltpu.get_barrier_semaphore()
    peers = peers_of(("rec", "attr"))
    for r, a in peers:
        pl.semaphore_signal(barrier, inc=1, device_id={"rec": r, "attr": a}, device_id_type=MESH)

    def at(k):
        return places.at[k:k + 1]

    loads[0].wait()
    loads[1].wait()
    pack(c_send, moved(at(0), rows_of(cells, flat)), few)
    pl.semaphore_wait(barrier, len(peers))
    c_copies = start_swap(("attr",), c_send, c_got, c_sems)
    loads[2].wait()
    pack(g_send, moved(at(1), rows_of(cot, flat)), few)
    g_copies = start_swap(("rec",), g_send, g_got, g_sems)
    for k in range(3, len(pairs)):
        loads[k].wait()
    for k, i in enumerate(KEPT):
        hots[k] = mover(at(i))
    settle(c_copies)
    x_a[...] = unpack(c_got, flat, few)
    _, mixed, first = attend(x_a, qkva, outa[...], qkv_a, p_a, acc, n_a, size_a, None, None)
    mixed_a[...] = mixed
    pack(f_send, dot(hots[0], first), few)
    f_copies = start_swap(("rec", "attr"), f_send, f_got, f_sems)

    row = lax.broadcasted_iota(jnp.int32, (size_s, size_s), 0)
    column = lax.broadcasted_iota(jnp.int32, (size_s, size_s), 1)
    same = None
    for s in range(size_s // length):
        low, high = s * length, (s + 1) * length
        inside = (row >= low) & (row < high) & (column >= low) & (column < high)
        same = inside if same is None else same | inside
    tiled = jnp.concatenate([split[...].astype(F32)] * (size_s // length), axis=1)
    bias[...] = jnp.where(same, tiled, 0.0).T
    settle(g_copies)
    g_s[...] = moved(at(4), unpack(g_got, flat, few)).astype(BF16)
    settle(f_copies)
    x_s[...] = dot(hots[1], unpack(f_got, flat, few)).astype(BF16)
    _, mixed, second = attend(x_s, qkvs, outs[...], qkv_s, p_s, acc, n_s, size_s, bias, (hat_s, scale_s))
    saves = []
    starts = [sum(COUNTS[:k]) for k in range(4)]
    ffn1, ffn2, samp, attr = (
        total_steps(k > 1, saves, totals_h, save_sems.at[k], grads, totals, starts[k], COUNTS[k], *sums[4 * k:4 * k + 4]) for k in range(4)
    )
    hat, scale = norm(second.astype(F32))
    normed = hat.astype(BF16)
    g = g_s[...]
    for c in range(up.shape[1] // E):
        w_up = up[:, c * E:(c + 1) * E]
        pre = dot(normed, w_up)
        cdf = 0.5 * (1.0 + lax.erf(pre * (1.0 / math.sqrt(2.0))))
        hidden = (pre * cdf).astype(BF16)
        slope = cdf + pre * (jnp.exp(pre * pre * -0.5) * (1.0 / math.sqrt(2.0 * math.pi)))
        dh = dot(g, down[:, c * E:(c + 1) * E]).astype(BF16).astype(F32)
        dpre = (dh * slope).astype(BF16)
        put(grads, UP[c], dot(normed, dpre, TN))
        put(grads, DOWN[c], dot(g, hidden, TN))
        part = dot(dpre, w_up, NT)
        if c == 0:
            dn_s[...] = part
        else:
            dn_s[...] += part
        if c == 1:
            next(ffn1)
    next(ffn2)
    next(ffn1)
    dn = dn_s[...].astype(BF16).astype(F32)
    g = (g.astype(F32) + norm_back(hat, scale, dn)).astype(BF16)

    def go(*groups):
        def step():
            for group in groups:
                next(group)
        return step

    heads_back(
        g, outs[...], qkv_s, p_s, acc, dm_s, n_s, size_s, {1: go(ffn2)},
    )
    for t in range(3):
        d_s[t] = acc[t].T.astype(BF16)
    back = input_back(hat_s[...], scale_s[...], g, d_s, qkvs)
    pack(b_send, dot(hots[2], back), few)
    b_copies = start_swap(("rec", "attr"), b_send, b_got, b_sems)
    put(grads, starts[2] + 3, dot(mixed, g, TN))
    weights_back(hat_s[...].astype(BF16), d_s, grads, starts[2])
    go(samp, ffn1, samp, ffn2)()
    hat_s[...], scale_s[...] = norm(x_a[...].astype(F32))
    settle(b_copies)
    g = dot(hots[3], unpack(b_got, flat, few)).astype(BF16)
    put(grads, starts[3] + 3, dot(mixed_a[...], g, TN))
    heads_back(
        g, outa[...], qkv_a, p_a, acc, dm_s, n_a, size_a, {1: go(ffn1), 2: go(samp), 3: go(ffn2), 5: go(ffn1)},
    )
    for t in range(3):
        d_s[t] = acc[t].T.astype(BF16)
    hat = hat_s[...]
    weights_back(hat.astype(BF16), d_s, grads, starts[3])
    next(attr)
    back = input_back(hat, scale_s[...], g, d_s, qkva)
    pack(o_send, back.astype(F32), few)
    o_copies = start_swap(("attr",), o_send, o_got, o_sems)

    def cells_back():
        settle(o_copies)
        save = pltpu.make_async_copy(o_got, o_h, save_sems.at[len(COUNTS)])
        save.start()
        saves.append(save)
        yield

    cells_out = cells_back()
    for steps in (attr, ffn2, ffn1, samp, attr, ffn2, samp, cells_out, attr, attr):
        next(steps)
    for save in saves:
        save.wait()


def finish_kernel(
    factor, few, tokens_h, places_h, total_h, cells_h, qa_h, oa_h, qs_h, os_h, gu_h, gd_h,
    tokens, places, total, cells, qa, oa, qs, os, gu, gd, sems, out_sems, flat, out_flat, tmp,
):
    loads = [
        pltpu.make_async_copy(src, dst, sems.at[k])
        for k, (src, dst) in enumerate(
            [(total_h.at[pl.ds(4 * k, 4)], total.at[pl.ds(4 * k, 4)]) for k in range(4)]
            + [(places_h, places), (tokens_h, tokens)]
        )
    ]
    for load in loads:
        load.start()
    rows = cells.shape[0]

    def block(b):
        part = total.shape[2]
        for r in range(total.shape[1]):
            tmp[b, r * part:(r + 1) * part] = total[b, r].astype(F32) * factor
        side = tmp[b]
        return jnp.concatenate([side[:, :E], side[:, E:]], axis=0)

    stores = []

    def store(src, dst):
        copy = pltpu.make_async_copy(src, dst, out_sems.at[len(stores)])
        copy.start()
        stores.append(copy)

    loads[0].wait()
    loads[1].wait()
    gu[...] = jnp.concatenate([block(c) for c in UP], axis=1)
    store(gu, gu_h)
    gd[...] = jnp.concatenate([block(c) for c in DOWN], axis=1)
    store(gd, gd_h)
    for ref, dst, side, side_h, k in ((qs, qs_h, os, os_h, 2), (qa, qa_h, oa, oa_h, 3)):
        loads[k].wait()
        ref[...] = jnp.concatenate([block(4 * k + t) for t in range(3)], axis=1)
        store(ref, dst)
        side[...] = block(4 * k + 3)
        store(side, side_h)
    loads[4].wait()
    loads[5].wait()
    out_flat[...] = moved(places.at[7:8], unpack(tokens, flat, few))
    for a in range(0, cells.shape[1] // E, 2):
        pair = [out_flat[(a + k) * rows:(a + k + 1) * rows] for k in range(2)]
        cells[:, a * E:(a + 2) * E] = jnp.concatenate(pair, axis=1).astype(BF16)
    store(cells, cells_h)
    for copy in stores:
        copy.wait()


def local(
    cells, cotangent, qkv_attr, out_attr, qkv_samp, out_samp, up_weight, down_weight, train_split
):
    n_rec, n_attr = lax.axis_size("rec"), lax.axis_size("attr")
    rows, cols = cells.shape[0], cells.shape[1] // E
    tokens = rows * cols
    width = cols * n_attr
    length = rows * n_rec
    few = rows // n_attr
    thin = cols // n_rec
    size = length * max(1, min(256 // length, thin))
    places = jnp.asarray(np.stack([
        place((cols, n_attr, few), (2, 1, 0)),
        place((n_rec, thin, n_attr, few), (3, 0, 1, 2)),
        place((few, n_attr, n_rec, thin), (0, 2, 1, 3)),
        place((few, n_rec, n_attr, thin), (3, 1, 2, 0)),
        place((few, n_rec, thin, n_attr), (2, 1, 3, 0)),
        place((thin, n_rec, n_attr, few), (3, 1, 2, 0)),
        place((few, n_rec, n_attr, thin), (0, 2, 1, 3)),
        place((few, n_attr, cols), (2, 1, 0)),
    ]))
    split = train_split[None, :]
    all_devices = n_rec * n_attr
    part = E // 2 // n_rec
    n_x = n_attr // 2

    def shape(*dims, dtype=BF16):
        return jax.ShapeDtypeStruct(dims, dtype)

    def vmem(*dims, dtype=BF16):
        return pltpu.VMEM(dims, dtype)

    args = (
        cells, cotangent, qkv_attr, out_attr, qkv_samp, out_samp, up_weight, down_weight.T, split, places
    )
    c_buf = vmem(n_attr, cols, few * E)
    g_buf = vmem(n_rec, thin * n_attr, few * E)
    f_buf = vmem(all_devices, thin, few * E)
    table = vmem(tokens, E)
    sums = []
    for count in COUNTS:
        h1 = count // 2
        h2 = h1 // n_x
        sums += [
            vmem(h1, n_rec, part, 2 * E), vmem(n_rec * n_x - 1, h2, part, 2 * E),
            vmem(h1, n_rec, part, 2 * E), pltpu.SemaphoreType.DMA((2, 2 * n_rec * n_x)),
        ]
    o_got, totals = pl.pallas_call(
        functools.partial(layer_kernel, width, size, length, few),
        out_shape=[shape(n_attr, cols, few * E), shape(BLOCKS, n_rec, part, 2 * E)],
        in_specs=[HBM] * len(args),
        out_specs=[HBM] * 2,
        scratch_shapes=[
            c_buf, vmem(BLOCKS, n_rec, part, 2 * E), pltpu.SemaphoreType.DMA((len(COUNTS) + 1,)),
        ]
        + [pltpu.VMEM(a.shape, a.dtype) for a in args]
        + [
            pltpu.SemaphoreType.DMA((len(args),)),
            vmem(tokens, E, dtype=F32), c_buf, c_buf, g_buf, g_buf, f_buf, f_buf, f_buf, f_buf, c_buf,
            table, table, vmem(3, E, tokens), vmem(tokens // width, HEADS, width, width, dtype=F32),
            table, table, vmem(3, E, tokens), vmem(tokens // size, HEADS, size, size, dtype=F32),
            vmem(3, E, tokens, dtype=F32), vmem(3, tokens, E), vmem(E, tokens), vmem(tokens, E, dtype=F32),
            vmem(tokens, E, dtype=F32), vmem(tokens, 1, dtype=F32), vmem(len(KEPT), tokens, tokens),
            vmem(size, size, dtype=F32), vmem(BLOCKS, n_rec, part, 2 * E),
        ]
        + [
            pltpu.SemaphoreType.DMA((2, n))
            for n in (n_attr, n_rec, all_devices, all_devices, n_attr)
        ]
        + sums,
        compiler_params=pltpu.CompilerParams(
            collective_id=0, has_side_effects=True, vmem_limit_bytes=67043328
        ),
    )(*args)
    outs = [
        shape(rows, cols * E), shape(E, 3 * E, dtype=F32), shape(E, E, dtype=F32),
        shape(E, 3 * E, dtype=F32), shape(E, E, dtype=F32),
        shape(E, 4 * E, dtype=F32), shape(E, 4 * E, dtype=F32),
    ]
    last = (o_got, places, totals)
    out = pl.pallas_call(
        functools.partial(finish_kernel, 1.0 / math.sqrt(length * width), few),
        out_shape=outs,
        in_specs=[ANY] * 3,
        out_specs=[ANY] * len(outs),
        scratch_shapes=[pltpu.VMEM(a.shape, a.dtype) for a in (*last, *outs)]
        + [
            pltpu.SemaphoreType.DMA((6,)), pltpu.SemaphoreType.DMA((len(outs),)), vmem(tokens, E, dtype=F32), vmem(tokens, E, dtype=F32),
            vmem(BLOCKS, E // 2, 2 * E, dtype=F32),
        ],
        compiler_params=pltpu.CompilerParams(vmem_limit_bytes=67043328),
    )(*last)
    return (*out[:6], out[6].T)


def solution(mesh):
    both = P(("groups", "rec"), "attr")
    in_specs = (both, both, P(), P(), P(), P(), P(), P(), P("groups"))
    out_specs = (both,) + (P("groups", None),) * 6
    return jax.shard_map(local, mesh=mesh, in_specs=in_specs, out_specs=out_specs, check_vma=False)
```

```python
import functools
import math

import jax
import jax.numpy as jnp
import numpy as np
from jax import lax
from jax.experimental import pallas as pl
from jax.experimental.pallas import tpu as pltpu
from jax.sharding import PartitionSpec as P

E = 192
HEADS = 6
HD = E // HEADS
SCALE = 1.0 / math.sqrt(HD)
BLOCKS = 16
F32 = jnp.float32
BF16 = jnp.bfloat16
MESH = pl.DeviceIdType.MESH
NN = (((1,), (0,)), ((), ()))
NT = (((1,), (1,)), ((), ()))
TN = (((0,), (0,)), ((), ()))
VMEM = pl.BlockSpec(memory_space=pltpu.VMEM)
ANY = pl.BlockSpec(memory_space=pl.ANY)
HBM = pl.BlockSpec(memory_space=pltpu.HBM)


def dot(a, b, form=NN):
    return lax.dot_general(a, b, form, preferred_element_type=F32)


def place(sizes, order):
    index = np.arange(math.prod(sizes)).reshape(sizes).transpose(order).reshape(-1)
    there = np.empty_like(index)
    there[index] = np.arange(index.size)
    return there.astype(np.int32)


def mover(where_ref):
    n = where_ref.shape[1]
    hot = lax.broadcasted_iota(jnp.int32, (n, n), 0) == where_ref[...]
    return jnp.where(hot, 1.0, 0.0).astype(BF16)


def moved(where_ref, x):
    return dot(mover(where_ref), x)


def put(ref, b, value):
    pieces, part = ref.shape[1], ref.shape[2]
    side = jnp.concatenate([value[: E // 2], value[E // 2:]], axis=1)
    for r in range(pieces):
        ref[b, r] = side[r * part:(r + 1) * part].astype(BF16)


def pack(ref, value, few):
    run = value.shape[0] // few
    pieces, part = ref.shape[0], ref.shape[1]
    side = jnp.concatenate([value[k * run:(k + 1) * run] for k in range(few)], axis=1)
    for r in range(pieces):
        ref[r] = side[r * part:(r + 1) * part].astype(BF16)


def unpack(ref, flat, few):
    pieces, part = ref.shape[0], ref.shape[1]
    run = pieces * part
    for r in range(pieces):
        side = ref[r].astype(F32)
        for k in range(few):
            flat[k * run + r * part:k * run + (r + 1) * part] = side[:, k * E:(k + 1) * E]
    return flat[...].astype(BF16)


def norm(x):
    center = x - jnp.mean(x, axis=-1, keepdims=True)
    scale = lax.rsqrt(jnp.mean(center * center, axis=-1, keepdims=True) + 1e-05)
    return center * scale, scale


def norm_back(hat, scale, grad):
    return scale * (
        grad
        - jnp.mean(grad, axis=-1, keepdims=True)
        - hat * jnp.mean(grad * hat, axis=-1, keepdims=True)
    )


def attend(x_ref, turned, out, qkv_s, p_s, acc, n, size, bias, kept):
    hat, scale = norm(x_ref[...].astype(F32))
    normed = hat.astype(BF16)
    if kept is not None:
        kept[0][...], kept[1][...] = hat, scale
    for t in range(3):
        qkv_s[t] = dot(turned[t], normed, NT).astype(BF16)

    def head(h):
        rows = pl.ds(h * HD, HD)
        for b in range(n):
            cols = pl.ds(b * size, size)
            s = dot(qkv_s[1, rows, cols], qkv_s[0, rows, cols], TN) * SCALE
            if bias is not None:
                s = jnp.where(bias[...] > 0, s, -1e30)
            e = jnp.exp(s - jnp.max(s, axis=0, keepdims=True))
            p = e * (1.0 / jnp.sum(e, axis=0, keepdims=True))
            p_s[b, h] = p
            acc[0, rows, cols] = dot(qkv_s[2, rows, cols], p.astype(BF16))

    for h in range(HEADS):
        head(h)
    mixed = acc[0].astype(BF16)
    return mixed, (x_ref[...].astype(F32) + dot(mixed.T, out)).astype(BF16)


def heads_back(g, out, qkv_s, p_s, acc, dm_s, n, size, between):
    dm_s[...] = dot(out, g, NT).astype(BF16)

    def head(h):
        rows = pl.ds(h * HD, HD)
        for b in range(n):
            cols = pl.ds(b * size, size)
            dm = dm_s[rows, cols]
            p = p_s[b, h]
            dp = dot(qkv_s[2, rows, cols], dm, TN).astype(BF16).astype(F32)
            ds = (p * (dp - jnp.sum(dp * p, axis=0, keepdims=True)) * SCALE).astype(BF16)
            acc[0, rows, cols] = dot(qkv_s[1, rows, cols], ds)
            acc[1, rows, cols] = dot(qkv_s[0, rows, cols], ds, NT)
            acc[2, rows, cols] = dot(dm, p.astype(BF16), NT)

    for h in range(HEADS):
        head(h)
        between.get(h, lambda: None)()


def weights_back(normed, d_s, grads, first):
    for t in range(3):
        put(grads, first + t, dot(normed, d_s[t], NT))


def input_back(hat, scale, g, d_s, qkv):
    dn = None
    for t in range(3):
        part = dot(qkv[:, t * E:(t + 1) * E], d_s[t])
        dn = part if dn is None else dn + part
    return (g.astype(F32) + norm_back(hat, scale, dn.astype(BF16).T.astype(F32))).astype(BF16)


def rows_of(cells, flat):
    rows = cells.shape[0]
    for a in range(cells.shape[1] // E):
        flat[a * rows:(a + 1) * rows] = cells[:, a * E:(a + 1) * E].astype(F32)
    return flat[...].astype(BF16)


def shifts_of(axes):
    sizes = [lax.axis_size(a) for a in axes]
    return [s for s in np.ndindex(*sizes) if any(s)], sizes


def peers_of(axes):
    shifts, sizes = shifts_of(axes)
    me = [lax.axis_index(a) for a in axes]
    return [[lax.rem(m + d, n) for m, d, n in zip(me, s, sizes)] for s in shifts]


def far_first(axis):
    n, me = lax.axis_size(axis), lax.axis_index(axis)
    low = 2 * me < n
    order = []
    for i in range(n - 1):
        down = n - 1 - i
        to = jnp.where(low, jnp.where(down <= me, down - 1, down), jnp.where(i >= me, i + 1, i))
        order.append((to, lax.rem(to - me + n, n)))
    return order


def ordered(axes):
    if axes[0] != "rec":
        return [(to, k) for k, to in enumerate(peers_of(axes))]
    if len(axes) == 1:
        return [([to], d - 1) for to, d in far_first("rec")]
    rec, attr, n = lax.axis_index("rec"), lax.axis_index("attr"), lax.axis_size("attr")
    turn = sorted(range(n), key=lambda c: -min(c, n - c))
    far = [([to, lax.rem(attr + c, n)], d * n + c - 1) for to, d in far_first("rec") for c in turn]
    return far + [([rec, lax.rem(attr + c, n)], c - 1) for c in turn if c]


def start_swap(axes, src, dst, sems):
    _, sizes = shifts_of(axes)

    def flat(where):
        number = where[0]
        for w, n in zip(where[1:], sizes[1:]):
            number = number * n + w
        return number

    me = flat([lax.axis_index(a) for a in axes])
    copies = []
    for to, k in ordered(axes):
        copy = pltpu.make_async_remote_copy(
            src_ref=src.at[flat(to)],
            dst_ref=dst.at[me],
            send_sem=sems.at[0, k],
            recv_sem=sems.at[1, k],
            device_id=dict(zip(axes, to)),
            device_id_type=MESH,
        )
        copy.start()
        copies.append(copy)
    dst[me] = src[me]
    return copies


def settle(copies):
    for copy in copies:
        copy.wait()


def total_steps(wide, saves, kept, save_sem, buf, out, first, count, r1, r2, s1, sems):
    rec, attr = lax.axis_index("rec"), lax.axis_index("attr")
    n_rec, n_x = lax.axis_size("rec"), lax.axis_size("attr") // 2
    half, x = lax.rem(attr, 2), lax.div(attr, 2)
    h1 = count // 2
    h2 = h1 // n_x
    base = first + half * h1 + x * h2

    def push(src, dst, device, k):
        copy = pltpu.make_async_remote_copy(
            src_ref=src, dst_ref=dst, send_sem=sems.at[0, k], recv_sem=sems.at[1, k],
            device_id=device, device_id_type=MESH,
        )
        copy.start()
        return copy

    partner = {"attr": x * 2 + 1 - half}
    turn = range(n_x - 1, -1, -1)
    chips = [(to, lax.rem(x + c, n_x), d * n_x + c) for to, d in far_first("rec") for c in turn]
    chips += [(rec, lax.rem(x + c, n_x), c) for c in turn if c]
    many = n_rec * n_x
    copies = [push(buf.at[pl.ds(first + (1 - half) * h1, h1)], r1, partner, 0)]
    yield
    settle(copies)
    for b in range(h1):
        s1[b] = (buf[first + half * h1 + b].astype(F32) + r1[b].astype(F32)).astype(BF16)
    copies = [
        push(s1.at[pl.ds(c * h2, h2), r], r2.at[k - 1], {"rec": r, "attr": c * 2 + half}, k)
        for r, c, k in chips
    ]
    yield
    settle(copies)
    for b in range(h2):
        value = s1[x * h2 + b, rec].astype(F32)
        for k in range(many - 1):
            value += r2[k, b].astype(F32)
        out[base + b, rec] = value.astype(BF16)
    own = out.at[pl.ds(base, h2), rec]
    if wide:
        copies = [push(own, own, {"rec": r, "attr": c * 2 + half}, many - 1 + k) for r, c, k in chips]
    else:
        copies = [push(own, own, {"rec": to}, many - 1 + d) for to, d in far_first("rec")]
        yield
        settle(copies)
        own = out.at[pl.ds(base, h2)]
        copies = [
            push(own, own, {"attr": lax.rem(x + c, n_x) * 2 + half}, many + n_rec - 2 + c)
            for c in range(1, n_x)
        ]
    yield
    settle(copies)
    own = out.at[pl.ds(first + half * h1, h1)]
    copies = [push(own, own, partner, 2 * many - 1)]
    yield
    settle(copies)
    group = pl.ds(first, count)
    save = pltpu.make_async_copy(out.at[group], kept.at[group], save_sem)
    save.start()
    saves.append(save)
    yield


COUNTS = (4, 4, 4, 4)
KEPT = (2, 3, 5, 6)
UP = (0, 1, 4, 5)
DOWN = (2, 3, 6, 7)


def layer_kernel(
    size_a, size_s, length, few,
    cells_h, cot_h, qkva_h, outa_h, qkvs_h, outs_h, up_h, down_h, split_h, place_h,
    o_h, totals_h,
    o_got, totals, save_sems, cells, cot, qkva, outa, qkvs, outs, up, down, split, places, in_sems,
    flat, c_send, c_got, g_send, g_got, f_send, f_got, b_send, b_got, o_send,
    x_a, mixed_a, qkv_a, p_a, x_s, g_s, qkv_s, p_s, acc, d_s, dm_s, dn_s, hat_s, scale_s, hots, turned, g_turned, mixed_s, bias, grads,
    c_sems, g_sems, f_sems, b_sems, o_sems, *sums,
):
    tokens = flat.shape[0]
    n_a, n_s = tokens // size_a, tokens // size_s
    loads = {}
    pairs = (
        (cells_h, cells), (place_h, places), (cot_h, cot), (qkva_h, qkva), (outa_h, outa),
        (split_h, split), (qkvs_h, qkvs), (outs_h, outs), (up_h, up), (down_h, down),
    )
    for k, (src, dst) in enumerate(pairs):
        loads[k] = pltpu.make_async_copy(src, dst, in_sems.at[k])
        loads[k].start()
    barrier = pltpu.get_barrier_semaphore()
    peers = peers_of(("rec", "attr"))
    for r, a in peers:
        pl.semaphore_signal(barrier, inc=1, device_id={"rec": r, "attr": a}, device_id_type=MESH)

    def at(k):
        return places.at[k:k + 1]

    loads[0].wait()
    loads[1].wait()
    pack(c_send, moved(at(0), rows_of(cells, flat)), few)
    pl.semaphore_wait(barrier, len(peers))
    c_copies = start_swap(("attr",), c_send, c_got, c_sems)
    loads[2].wait()
    pack(g_send, moved(at(1), rows_of(cot, flat)), few)
    g_copies = start_swap(("rec",), g_send, g_got, g_sems)
    for k in range(3, len(pairs)):
        loads[k].wait()
    for k, i in enumerate(KEPT):
        hots[k] = mover(at(i))
    for k, w in enumerate((qkva, qkvs)):
        for t in range(3):
            turned[k, t] = w[:, t * E:(t + 1) * E].T
    settle(c_copies)
    x_a[...] = unpack(c_got, flat, few)
    mixed, first = attend(x_a, turned.at[0], outa[...], qkv_a, p_a, acc, n_a, size_a, None, None)
    mixed_a[...] = mixed
    pack(f_send, dot(hots[0], first), few)
    f_copies = start_swap(("rec", "attr"), f_send, f_got, f_sems)

    row = lax.broadcasted_iota(jnp.int32, (size_s, size_s), 0)
    column = lax.broadcasted_iota(jnp.int32, (size_s, size_s), 1)
    same = None
    for s in range(size_s // length):
        low, high = s * length, (s + 1) * length
        inside = (row >= low) & (row < high) & (column >= low) & (column < high)
        same = inside if same is None else same | inside
    tiled = jnp.concatenate([split[...].astype(F32)] * (size_s // length), axis=1)
    bias[...] = jnp.where(same, tiled, 0.0).T
    settle(g_copies)
    g_s[...] = moved(at(4), unpack(g_got, flat, few)).astype(BF16)
    g_turned[...] = g_s[...].T
    settle(f_copies)
    x_s[...] = dot(hots[1], unpack(f_got, flat, few)).astype(BF16)
    mixed_s[...], second = attend(x_s, turned.at[1], outs[...], qkv_s, p_s, acc, n_s, size_s, bias, (hat_s, scale_s))
    saves = []
    starts = [sum(COUNTS[:k]) for k in range(4)]
    ffn1, ffn2, samp, attr = (
        total_steps(k > 1, saves, totals_h, save_sems.at[k], grads, totals, starts[k], COUNTS[k], *sums[4 * k:4 * k + 4]) for k in range(4)
    )
    hat, scale = norm(second.astype(F32))
    normed = hat.astype(BF16)
    normed_turned = normed.T
    g = g_s[...]
    for c in range(up.shape[1] // E):
        w_up = up[:, c * E:(c + 1) * E]
        pre = dot(normed, w_up)
        cdf = 0.5 * (1.0 + lax.erf(pre * (1.0 / math.sqrt(2.0))))
        hidden = (pre * cdf).astype(BF16)
        slope = cdf + pre * (jnp.exp(pre * pre * -0.5) * (1.0 / math.sqrt(2.0 * math.pi)))
        dh = dot(g, down[:, c * E:(c + 1) * E]).astype(BF16).astype(F32)
        dpre = (dh * slope).astype(BF16)
        put(grads, UP[c], dot(normed_turned, dpre))
        put(grads, DOWN[c], dot(g_turned[...], hidden))
        part = dot(dpre, w_up, NT)
        if c == 0:
            dn_s[...] = part
        else:
            dn_s[...] += part
        if c == 1:
            next(ffn1)
    next(ffn2)
    next(ffn1)
    dn = dn_s[...].astype(BF16).astype(F32)
    g = (g.astype(F32) + norm_back(hat, scale, dn)).astype(BF16)

    def go(*groups):
        def step():
            for group in groups:
                next(group)
        return step

    heads_back(
        g, outs[...], qkv_s, p_s, acc, dm_s, n_s, size_s, {1: go(ffn2)},
    )
    for t in range(3):
        d_s[t] = acc[t].astype(BF16)
    back = input_back(hat_s[...], scale_s[...], g, d_s, qkvs)
    pack(b_send, dot(hots[2], back), few)
    b_copies = start_swap(("rec", "attr"), b_send, b_got, b_sems)
    put(grads, starts[2] + 3, dot(mixed_s[...], g))
    weights_back(hat_s[...].astype(BF16).T, d_s, grads, starts[2])
    go(samp, ffn1, samp, ffn2)()
    hat_s[...], scale_s[...] = norm(x_a[...].astype(F32))
    g_turned[...] = hat_s[...].astype(BF16).T
    settle(b_copies)
    g = dot(hots[3], unpack(b_got, flat, few)).astype(BF16)
    put(grads, starts[3] + 3, dot(mixed_a[...], g))
    heads_back(
        g, outa[...], qkv_a, p_a, acc, dm_s, n_a, size_a, {1: go(ffn1), 2: go(samp), 3: go(ffn2), 5: go(ffn1)},
    )
    for t in range(3):
        d_s[t] = acc[t].astype(BF16)
    hat = hat_s[...]
    weights_back(g_turned[...], d_s, grads, starts[3])
    next(attr)
    back = input_back(hat, scale_s[...], g, d_s, qkva)
    pack(o_send, back.astype(F32), few)
    o_copies = start_swap(("attr",), o_send, o_got, o_sems)

    def cells_back():
        settle(o_copies)
        save = pltpu.make_async_copy(o_got, o_h, save_sems.at[len(COUNTS)])
        save.start()
        saves.append(save)
        yield

    cells_out = cells_back()
    for steps in (attr, ffn2, ffn1, samp, attr, ffn2, samp, cells_out, attr, attr):
        next(steps)
    for save in saves:
        save.wait()


def finish_kernel(
    factor, few, tokens_h, places_h, total_h, cells_h, qa_h, oa_h, qs_h, os_h, gu_h, gd_h,
    tokens, places, total, cells, qa, oa, qs, os, gu, gd, sems, out_sems, flat, out_flat, tmp,
):
    loads = [
        pltpu.make_async_copy(src, dst, sems.at[k])
        for k, (src, dst) in enumerate(
            [(total_h.at[pl.ds(4 * k, 4)], total.at[pl.ds(4 * k, 4)]) for k in range(4)]
            + [(places_h, places), (tokens_h, tokens)]
        )
    ]
    for load in loads:
        load.start()
    rows = cells.shape[0]

    def block(b):
        part = total.shape[2]
        for r in range(total.shape[1]):
            tmp[b, r * part:(r + 1) * part] = total[b, r].astype(F32) * factor
        side = tmp[b]
        return jnp.concatenate([side[:, :E], side[:, E:]], axis=0)

    stores = []

    def store(src, dst):
        copy = pltpu.make_async_copy(src, dst, out_sems.at[len(stores)])
        copy.start()
        stores.append(copy)

    loads[0].wait()
    loads[1].wait()
    gu[...] = jnp.concatenate([block(c) for c in UP], axis=1)
    store(gu, gu_h)
    gd[...] = jnp.concatenate([block(c) for c in DOWN], axis=1)
    store(gd, gd_h)
    for ref, dst, side, side_h, k in ((qs, qs_h, os, os_h, 2), (qa, qa_h, oa, oa_h, 3)):
        loads[k].wait()
        ref[...] = jnp.concatenate([block(4 * k + t) for t in range(3)], axis=1)
        store(ref, dst)
        side[...] = block(4 * k + 3)
        store(side, side_h)
    loads[4].wait()
    loads[5].wait()
    out_flat[...] = moved(places.at[7:8], unpack(tokens, flat, few))
    for a in range(0, cells.shape[1] // E, 2):
        pair = [out_flat[(a + k) * rows:(a + k + 1) * rows] for k in range(2)]
        cells[:, a * E:(a + 2) * E] = jnp.concatenate(pair, axis=1).astype(BF16)
    store(cells, cells_h)
    for copy in stores:
        copy.wait()


def local(
    cells, cotangent, qkv_attr, out_attr, qkv_samp, out_samp, up_weight, down_weight, train_split
):
    n_rec, n_attr = lax.axis_size("rec"), lax.axis_size("attr")
    rows, cols = cells.shape[0], cells.shape[1] // E
    tokens = rows * cols
    width = cols * n_attr
    length = rows * n_rec
    few = rows // n_attr
    thin = cols // n_rec
    size = length * max(1, min(256 // length, thin))
    places = jnp.asarray(np.stack([
        place((cols, n_attr, few), (2, 1, 0)),
        place((n_rec, thin, n_attr, few), (3, 0, 1, 2)),
        place((few, n_attr, n_rec, thin), (0, 2, 1, 3)),
        place((few, n_rec, n_attr, thin), (3, 1, 2, 0)),
        place((few, n_rec, thin, n_attr), (2, 1, 3, 0)),
        place((thin, n_rec, n_attr, few), (3, 1, 2, 0)),
        place((few, n_rec, n_attr, thin), (0, 2, 1, 3)),
        place((few, n_attr, cols), (2, 1, 0)),
    ]))
    split = train_split[None, :]
    all_devices = n_rec * n_attr
    part = E // 2 // n_rec
    n_x = n_attr // 2

    def shape(*dims, dtype=BF16):
        return jax.ShapeDtypeStruct(dims, dtype)

    def vmem(*dims, dtype=BF16):
        return pltpu.VMEM(dims, dtype)

    args = (
        cells, cotangent, qkv_attr, out_attr, qkv_samp, out_samp, up_weight, down_weight.T, split, places
    )
    c_buf = vmem(n_attr, cols, few * E)
    g_buf = vmem(n_rec, thin * n_attr, few * E)
    f_buf = vmem(all_devices, thin, few * E)
    table = vmem(tokens, E)
    sums = []
    for count in COUNTS:
        h1 = count // 2
        h2 = h1 // n_x
        sums += [
            vmem(h1, n_rec, part, 2 * E), vmem(n_rec * n_x - 1, h2, part, 2 * E),
            vmem(h1, n_rec, part, 2 * E), pltpu.SemaphoreType.DMA((2, 2 * n_rec * n_x)),
        ]
    o_got, totals = pl.pallas_call(
        functools.partial(layer_kernel, width, size, length, few),
        out_shape=[shape(n_attr, cols, few * E), shape(BLOCKS, n_rec, part, 2 * E)],
        in_specs=[HBM] * len(args),
        out_specs=[HBM] * 2,
        scratch_shapes=[
            c_buf, vmem(BLOCKS, n_rec, part, 2 * E), pltpu.SemaphoreType.DMA((len(COUNTS) + 1,)),
        ]
        + [pltpu.VMEM(a.shape, a.dtype) for a in args]
        + [
            pltpu.SemaphoreType.DMA((len(args),)),
            vmem(tokens, E, dtype=F32), c_buf, c_buf, g_buf, g_buf, f_buf, f_buf, f_buf, f_buf, c_buf,
            table, vmem(E, tokens), vmem(3, E, tokens), vmem(tokens // width, HEADS, width, width, dtype=F32),
            table, table, vmem(3, E, tokens), vmem(tokens // size, HEADS, size, size, dtype=F32),
            vmem(3, E, tokens, dtype=F32), vmem(3, E, tokens), vmem(E, tokens), vmem(tokens, E, dtype=F32),
            vmem(tokens, E, dtype=F32), vmem(tokens, 1, dtype=F32), vmem(len(KEPT), tokens, tokens),
            vmem(2, 3, E, E), vmem(E, tokens), vmem(E, tokens),
            vmem(size, size, dtype=F32), vmem(BLOCKS, n_rec, part, 2 * E),
        ]
        + [
            pltpu.SemaphoreType.DMA((2, n))
            for n in (n_attr, n_rec, all_devices, all_devices, n_attr)
        ]
        + sums,
        compiler_params=pltpu.CompilerParams(
            collective_id=0, has_side_effects=True, vmem_limit_bytes=67043328
        ),
    )(*args)
    outs = [
        shape(rows, cols * E), shape(E, 3 * E, dtype=F32), shape(E, E, dtype=F32),
        shape(E, 3 * E, dtype=F32), shape(E, E, dtype=F32),
        shape(E, 4 * E, dtype=F32), shape(E, 4 * E, dtype=F32),
    ]
    last = (o_got, places, totals)
    out = pl.pallas_call(
        functools.partial(finish_kernel, 1.0 / math.sqrt(length * width), few),
        out_shape=outs,
        in_specs=[ANY] * 3,
        out_specs=[ANY] * len(outs),
        scratch_shapes=[pltpu.VMEM(a.shape, a.dtype) for a in (*last, *outs)]
        + [
            pltpu.SemaphoreType.DMA((6,)), pltpu.SemaphoreType.DMA((len(outs),)), vmem(tokens, E, dtype=F32), vmem(tokens, E, dtype=F32),
            vmem(BLOCKS, E // 2, 2 * E, dtype=F32),
        ],
        compiler_params=pltpu.CompilerParams(vmem_limit_bytes=67043328),
    )(*last)
    return (*out[:6], out[6].T)


def solution(mesh):
    both = P(("groups", "rec"), "attr")
    in_specs = (both, both, P(), P(), P(), P(), P(), P(), P("groups"))
    out_specs = (both,) + (P("groups", None),) * 6
    return jax.shard_map(local, mesh=mesh, in_specs=in_specs, out_specs=out_specs, check_vma=False)
```

```python
import functools
import math

import jax
import jax.numpy as jnp
import numpy as np
from jax import lax
from jax.experimental import pallas as pl
from jax.experimental.pallas import tpu as pltpu
from jax.sharding import PartitionSpec as P

E = 192
HEADS = 6
HD = E // HEADS
SCALE = 1.0 / math.sqrt(HD)
BLOCKS = 16
F32 = jnp.float32
BF16 = jnp.bfloat16
MESH = pl.DeviceIdType.MESH
NN = (((1,), (0,)), ((), ()))
NT = (((1,), (1,)), ((), ()))
TN = (((0,), (0,)), ((), ()))
VMEM = pl.BlockSpec(memory_space=pltpu.VMEM)
ANY = pl.BlockSpec(memory_space=pl.ANY)
HBM = pl.BlockSpec(memory_space=pltpu.HBM)


def dot(a, b, form=NN):
    return lax.dot_general(a, b, form, preferred_element_type=F32)


def place(sizes, order):
    index = np.arange(math.prod(sizes)).reshape(sizes).transpose(order).reshape(-1)
    there = np.empty_like(index)
    there[index] = np.arange(index.size)
    return there.astype(np.int32)


def mover(where_ref):
    n = where_ref.shape[1]
    hot = lax.broadcasted_iota(jnp.int32, (n, n), 0) == where_ref[...]
    return jnp.where(hot, 1.0, 0.0).astype(BF16)


def moved(where_ref, x):
    return dot(mover(where_ref), x)


def put(ref, b, value):
    pieces, part = ref.shape[1], ref.shape[2]
    side = jnp.concatenate([value[: E // 2], value[E // 2:]], axis=1)
    for r in range(pieces):
        ref[b, r] = side[r * part:(r + 1) * part].astype(BF16)


def pack(ref, value, few):
    run = value.shape[0] // few
    pieces, part = ref.shape[0], ref.shape[1]
    side = jnp.concatenate([value[k * run:(k + 1) * run] for k in range(few)], axis=1)
    for r in range(pieces):
        ref[r] = side[r * part:(r + 1) * part].astype(BF16)


def unpack(ref, flat, few):
    pieces, part = ref.shape[0], ref.shape[1]
    run = pieces * part
    for r in range(pieces):
        side = ref[r].astype(F32)
        for k in range(few):
            flat[k * run + r * part:k * run + (r + 1) * part] = side[:, k * E:(k + 1) * E]
    return flat[...].astype(BF16)


def norm(x):
    center = x - jnp.mean(x, axis=-1, keepdims=True)
    scale = lax.rsqrt(jnp.mean(center * center, axis=-1, keepdims=True) + 1e-05)
    return center * scale, scale


def norm_back(hat, scale, grad):
    return scale * (
        grad
        - jnp.mean(grad, axis=-1, keepdims=True)
        - hat * jnp.mean(grad * hat, axis=-1, keepdims=True)
    )


def attend(x_ref, turned, out, qkv_s, p_s, acc, n, size, bias, kept):
    hat, scale = norm(x_ref[...].astype(F32))
    normed = hat.astype(BF16)
    if kept is not None:
        kept[0][...], kept[1][...] = hat, scale
    for t in range(3):
        qkv_s[t] = dot(turned[t], normed, NT).astype(BF16)

    def head(h):
        rows = pl.ds(h * HD, HD)
        for b in range(n):
            cols = pl.ds(b * size, size)
            s = dot(qkv_s[1, rows, cols], qkv_s[0, rows, cols], TN) * SCALE
            if bias is not None:
                s = jnp.where(bias[...] > 0, s, -1e30)
            e = jnp.exp(s - jnp.max(s, axis=0, keepdims=True))
            p = e * (1.0 / jnp.sum(e, axis=0, keepdims=True))
            p_s[b, h] = p
            acc[0, rows, cols] = dot(qkv_s[2, rows, cols], p.astype(BF16))

    for h in range(HEADS):
        head(h)
    mixed = acc[0].astype(BF16)
    return mixed, (x_ref[...].astype(F32) + dot(mixed.T, out)).astype(BF16)


def heads_back(g, out, qkv_s, p_s, acc, dm_s, n, size, between):
    dm_s[...] = dot(out, g, NT).astype(BF16)

    def head(h):
        rows = pl.ds(h * HD, HD)
        for b in range(n):
            cols = pl.ds(b * size, size)
            dm = dm_s[rows, cols]
            p = p_s[b, h]
            dp = dot(qkv_s[2, rows, cols], dm, TN).astype(BF16).astype(F32)
            ds = (p * (dp - jnp.sum(dp * p, axis=0, keepdims=True)) * SCALE).astype(BF16)
            acc[0, rows, cols] = dot(qkv_s[1, rows, cols], ds)
            acc[1, rows, cols] = dot(qkv_s[0, rows, cols], ds, NT)
            acc[2, rows, cols] = dot(dm, p.astype(BF16), NT)

    for h in range(HEADS):
        head(h)
        between.get(h, lambda: None)()


def weights_back(normed, d_s, grads, first):
    for t in range(3):
        put(grads, first + t, dot(normed, d_s[t], NT))


def input_back(hat, scale, g, d_s, qkv):
    dn = None
    for t in range(3):
        part = dot(qkv[:, t * E:(t + 1) * E], d_s[t])
        dn = part if dn is None else dn + part
    return (g.astype(F32) + norm_back(hat, scale, dn.astype(BF16).T.astype(F32))).astype(BF16)


def rows_of(cells, flat):
    rows = cells.shape[0]
    for a in range(cells.shape[1] // E):
        flat[a * rows:(a + 1) * rows] = cells[:, a * E:(a + 1) * E].astype(F32)
    return flat[...].astype(BF16)


def shifts_of(axes):
    sizes = [lax.axis_size(a) for a in axes]
    return [s for s in np.ndindex(*sizes) if any(s)], sizes


def peers_of(axes):
    shifts, sizes = shifts_of(axes)
    me = [lax.axis_index(a) for a in axes]
    return [[lax.rem(m + d, n) for m, d, n in zip(me, s, sizes)] for s in shifts]


def far_first(axis):
    n, me = lax.axis_size(axis), lax.axis_index(axis)
    low = 2 * me < n
    order = []
    for i in range(n - 1):
        down = n - 1 - i
        to = jnp.where(low, jnp.where(down <= me, down - 1, down), jnp.where(i >= me, i + 1, i))
        order.append((to, lax.rem(to - me + n, n)))
    return order


def ordered(axes):
    if axes[0] != "rec":
        return [(to, k) for k, to in enumerate(peers_of(axes))]
    if len(axes) == 1:
        return [([to], d - 1) for to, d in far_first("rec")]
    rec, attr, n = lax.axis_index("rec"), lax.axis_index("attr"), lax.axis_size("attr")
    turn = sorted(range(n), key=lambda c: -min(c, n - c))
    far = [([to, lax.rem(attr + c, n)], d * n + c - 1) for to, d in far_first("rec") for c in turn]
    return far + [([rec, lax.rem(attr + c, n)], c - 1) for c in turn if c]


def start_swap(axes, src, dst, sems):
    _, sizes = shifts_of(axes)

    def flat(where):
        number = where[0]
        for w, n in zip(where[1:], sizes[1:]):
            number = number * n + w
        return number

    me = flat([lax.axis_index(a) for a in axes])
    copies = []
    for to, k in ordered(axes):
        copy = pltpu.make_async_remote_copy(
            src_ref=src.at[flat(to)],
            dst_ref=dst.at[me],
            send_sem=sems.at[0, k],
            recv_sem=sems.at[1, k],
            device_id=dict(zip(axes, to)),
            device_id_type=MESH,
        )
        copy.start()
        copies.append(copy)
    dst[me] = src[me]
    return copies


def settle(copies):
    for copy in copies:
        copy.wait()


def total_steps(wide, saves, kept, save_sem, buf, out, first, count, r1, r2, s1, sems):
    rec, attr = lax.axis_index("rec"), lax.axis_index("attr")
    n_rec, n_x = lax.axis_size("rec"), lax.axis_size("attr") // 2
    half, x = lax.rem(attr, 2), lax.div(attr, 2)
    h1 = count // 2
    h2 = h1 // n_x
    base = first + half * h1 + x * h2

    def push(src, dst, device, k):
        copy = pltpu.make_async_remote_copy(
            src_ref=src, dst_ref=dst, send_sem=sems.at[0, k], recv_sem=sems.at[1, k],
            device_id=device, device_id_type=MESH,
        )
        copy.start()
        return copy

    partner = {"attr": x * 2 + 1 - half}
    turn = range(n_x - 1, -1, -1)
    chips = [(to, lax.rem(x + c, n_x), d * n_x + c) for to, d in far_first("rec") for c in turn]
    chips += [(rec, lax.rem(x + c, n_x), c) for c in turn if c]
    many = n_rec * n_x
    copies = [push(buf.at[pl.ds(first + (1 - half) * h1, h1)], r1, partner, 0)]
    yield
    settle(copies)
    for b in range(h1):
        s1[b] = (buf[first + half * h1 + b].astype(F32) + r1[b].astype(F32)).astype(BF16)
    copies = [
        push(s1.at[pl.ds(c * h2, h2), r], r2.at[k - 1], {"rec": r, "attr": c * 2 + half}, k)
        for r, c, k in chips
    ]
    yield
    settle(copies)
    for b in range(h2):
        value = s1[x * h2 + b, rec].astype(F32)
        for k in range(many - 1):
            value += r2[k, b].astype(F32)
        out[base + b, rec] = value.astype(BF16)
    own = out.at[pl.ds(base, h2), rec]
    if wide:
        copies = [push(own, own, {"rec": r, "attr": c * 2 + half}, many - 1 + k) for r, c, k in chips]
    else:
        copies = [push(own, own, {"rec": to}, many - 1 + d) for to, d in far_first("rec")]
        yield
        settle(copies)
        own = out.at[pl.ds(base, h2)]
        copies = [
            push(own, own, {"attr": lax.rem(x + c, n_x) * 2 + half}, many + n_rec - 2 + c)
            for c in range(1, n_x)
        ]
    yield
    settle(copies)
    own = out.at[pl.ds(first + half * h1, h1)]
    copies = [push(own, own, partner, 2 * many - 1)]
    yield
    settle(copies)
    group = pl.ds(first, count)
    save = pltpu.make_async_copy(out.at[group], kept.at[group], save_sem)
    save.start()
    saves.append(save)
    yield


COUNTS = (4, 4, 4, 4)
KEPT = (2, 3, 5, 6)
UP = (0, 1, 4, 5)
DOWN = (2, 3, 6, 7)


def layer_kernel(
    size_a, size_s, length, few,
    cells_h, cot_h, qkva_h, outa_h, qkvs_h, outs_h, up_h, down_h, split_h, place_h,
    o_h, totals_h,
    o_got, totals, save_sems, cells, cot, qkva, outa, qkvs, outs, up, down, split, places, in_sems,
    flat, c_send, c_got, g_send, g_got, f_send, f_got, b_send, b_got, o_send,
    x_a, mixed_a, qkv_a, p_a, x_s, g_s, qkv_s, p_s, acc, d_s, dm_s, dn_s, hat_s, scale_s, hots, turned, g_turned, mixed_s, bias, grads,
    c_sems, g_sems, f_sems, b_sems, o_sems, *sums,
):
    tokens = flat.shape[0]
    n_a, n_s = tokens // size_a, tokens // size_s
    loads = {}
    pairs = (
        (cells_h, cells), (place_h, places), (cot_h, cot), (qkva_h, qkva), (outa_h, outa),
        (split_h, split), (qkvs_h, qkvs), (outs_h, outs), (up_h, up), (down_h, down),
    )
    for k, (src, dst) in enumerate(pairs):
        loads[k] = pltpu.make_async_copy(src, dst, in_sems.at[k])
        loads[k].start()
    barrier = pltpu.get_barrier_semaphore()
    peers = peers_of(("rec", "attr"))
    for r, a in peers:
        pl.semaphore_signal(barrier, inc=1, device_id={"rec": r, "attr": a}, device_id_type=MESH)

    def at(k):
        return places.at[k:k + 1]

    loads[0].wait()
    loads[1].wait()
    pack(c_send, moved(at(0), rows_of(cells, flat)), few)
    pl.semaphore_wait(barrier, len(peers))
    c_copies = start_swap(("attr",), c_send, c_got, c_sems)
    loads[2].wait()
    pack(g_send, moved(at(1), rows_of(cot, flat)), few)
    g_copies = start_swap(("rec",), g_send, g_got, g_sems)
    for k in range(3, len(pairs)):
        loads[k].wait()
    for k, i in enumerate(KEPT):
        hots[k] = mover(at(i))
    for k, w in enumerate((qkva, qkvs)):
        for t in range(3):
            turned[k, t] = w[:, t * E:(t + 1) * E].T
    settle(c_copies)
    x_a[...] = unpack(c_got, flat, few)
    mixed, first = attend(x_a, turned.at[0], outa[...], qkv_a, p_a, acc, n_a, size_a, None, None)
    mixed_a[...] = mixed
    pack(f_send, dot(hots[0], first), few)
    f_copies = start_swap(("rec", "attr"), f_send, f_got, f_sems)

    row = lax.broadcasted_iota(jnp.int32, (size_s, size_s), 0)
    column = lax.broadcasted_iota(jnp.int32, (size_s, size_s), 1)
    same = None
    for s in range(size_s // length):
        low, high = s * length, (s + 1) * length
        inside = (row >= low) & (row < high) & (column >= low) & (column < high)
        same = inside if same is None else same | inside
    tiled = jnp.concatenate([split[...].astype(F32)] * (size_s // length), axis=1)
    bias[...] = jnp.where(same, tiled, 0.0).T
    settle(g_copies)
    g_s[...] = moved(at(4), unpack(g_got, flat, few)).astype(BF16)
    g_turned[...] = g_s[...].T
    settle(f_copies)
    x_s[...] = dot(hots[1], unpack(f_got, flat, few)).astype(BF16)
    mixed_s[...], second = attend(x_s, turned.at[1], outs[...], qkv_s, p_s, acc, n_s, size_s, bias, (hat_s, scale_s))
    saves = []
    starts = [sum(COUNTS[:k]) for k in range(4)]
    ffn1, ffn2, samp, attr = (
        total_steps(k > 1, saves, totals_h, save_sems.at[k], grads, totals, starts[k], COUNTS[k], *sums[4 * k:4 * k + 4]) for k in range(4)
    )
    hat, scale = norm(second.astype(F32))
    normed = hat.astype(BF16)
    normed_turned = normed.T
    g = g_s[...]
    for c in range(up.shape[1] // E):
        w_up = up[:, c * E:(c + 1) * E]
        pre = dot(normed, w_up)
        cdf = 0.5 * (1.0 + lax.erf(pre * (1.0 / math.sqrt(2.0))))
        hidden = (pre * cdf).astype(BF16)
        slope = cdf + pre * (jnp.exp(pre * pre * -0.5) * (1.0 / math.sqrt(2.0 * math.pi)))
        dh = dot(g, down[:, c * E:(c + 1) * E]).astype(BF16).astype(F32)
        dpre = (dh * slope).astype(BF16)
        put(grads, UP[c], dot(normed_turned, dpre))
        put(grads, DOWN[c], dot(g_turned[...], hidden))
        part = dot(dpre, w_up, NT)
        if c == 0:
            dn_s[...] = part
        else:
            dn_s[...] += part
        if c == 1:
            next(ffn1)
    next(ffn2)
    next(ffn1)
    dn = dn_s[...].astype(BF16).astype(F32)
    g = (g.astype(F32) + norm_back(hat, scale, dn)).astype(BF16)

    def go(*groups):
        def step():
            for group in groups:
                next(group)
        return step

    heads_back(
        g, outs[...], qkv_s, p_s, acc, dm_s, n_s, size_s, {1: go(ffn2)},
    )
    for t in range(3):
        d_s[t] = acc[t].astype(BF16)
    back = input_back(hat_s[...], scale_s[...], g, d_s, qkvs)
    pack(b_send, dot(hots[2], back), few)
    b_copies = start_swap(("rec", "attr"), b_send, b_got, b_sems)
    put(grads, starts[2] + 3, dot(mixed_s[...], g))
    weights_back(hat_s[...].astype(BF16).T, d_s, grads, starts[2])
    go(samp, ffn1, samp, ffn2)()
    hat_s[...], scale_s[...] = norm(x_a[...].astype(F32))
    g_turned[...] = hat_s[...].astype(BF16).T
    settle(b_copies)
    g = dot(hots[3], unpack(b_got, flat, few)).astype(BF16)
    put(grads, starts[3] + 3, dot(mixed_a[...], g))
    heads_back(
        g, outa[...], qkv_a, p_a, acc, dm_s, n_a, size_a, {1: go(ffn1), 2: go(samp), 4: go(ffn2), 5: go(ffn1)},
    )
    for t in range(3):
        d_s[t] = acc[t].astype(BF16)
    hat = hat_s[...]
    weights_back(g_turned[...], d_s, grads, starts[3])
    next(attr)
    back = input_back(hat, scale_s[...], g, d_s, qkva)
    pack(o_send, back.astype(F32), few)
    o_copies = start_swap(("attr",), o_send, o_got, o_sems)

    def cells_back():
        settle(o_copies)
        save = pltpu.make_async_copy(o_got, o_h, save_sems.at[len(COUNTS)])
        save.start()
        saves.append(save)
        yield

    cells_out = cells_back()
    for steps in (attr, ffn2, ffn1, samp, attr, ffn2, samp, cells_out, attr, attr):
        next(steps)
    for save in saves:
        save.wait()


def finish_kernel(
    factor, few, tokens_h, places_h, total_h, cells_h, qa_h, oa_h, qs_h, os_h, gu_h, gd_h,
    tokens, places, total, cells, qa, oa, qs, os, gu, gd, sems, out_sems, flat, out_flat, tmp,
):
    loads = [
        pltpu.make_async_copy(src, dst, sems.at[k])
        for k, (src, dst) in enumerate(
            [(total_h.at[pl.ds(4 * k, 4)], total.at[pl.ds(4 * k, 4)]) for k in range(4)]
            + [(places_h, places), (tokens_h, tokens)]
        )
    ]
    for load in loads:
        load.start()
    rows = cells.shape[0]

    def block(b):
        part = total.shape[2]
        for r in range(total.shape[1]):
            tmp[b, r * part:(r + 1) * part] = total[b, r].astype(F32) * factor
        side = tmp[b]
        return jnp.concatenate([side[:, :E], side[:, E:]], axis=0)

    stores = []

    def store(src, dst):
        copy = pltpu.make_async_copy(src, dst, out_sems.at[len(stores)])
        copy.start()
        stores.append(copy)

    loads[0].wait()
    loads[1].wait()
    gu[...] = jnp.concatenate([block(c) for c in UP], axis=1)
    store(gu, gu_h)
    gd[...] = jnp.concatenate([block(c) for c in DOWN], axis=1)
    store(gd, gd_h)
    for ref, dst, side, side_h, k in ((qs, qs_h, os, os_h, 2), (qa, qa_h, oa, oa_h, 3)):
        loads[k].wait()
        ref[...] = jnp.concatenate([block(4 * k + t) for t in range(3)], axis=1)
        store(ref, dst)
        side[...] = block(4 * k + 3)
        store(side, side_h)
    loads[4].wait()
    loads[5].wait()
    out_flat[...] = moved(places.at[7:8], unpack(tokens, flat, few))
    for a in range(0, cells.shape[1] // E, 2):
        pair = [out_flat[(a + k) * rows:(a + k + 1) * rows] for k in range(2)]
        cells[:, a * E:(a + 2) * E] = jnp.concatenate(pair, axis=1).astype(BF16)
    store(cells, cells_h)
    for copy in stores:
        copy.wait()


def local(
    cells, cotangent, qkv_attr, out_attr, qkv_samp, out_samp, up_weight, down_weight, train_split
):
    n_rec, n_attr = lax.axis_size("rec"), lax.axis_size("attr")
    rows, cols = cells.shape[0], cells.shape[1] // E
    tokens = rows * cols
    width = cols * n_attr
    length = rows * n_rec
    few = rows // n_attr
    thin = cols // n_rec
    size = length * max(1, min(256 // length, thin))
    places = jnp.asarray(np.stack([
        place((cols, n_attr, few), (2, 1, 0)),
        place((n_rec, thin, n_attr, few), (3, 0, 1, 2)),
        place((few, n_attr, n_rec, thin), (0, 2, 1, 3)),
        place((few, n_rec, n_attr, thin), (3, 1, 2, 0)),
        place((few, n_rec, thin, n_attr), (2, 1, 3, 0)),
        place((thin, n_rec, n_attr, few), (3, 1, 2, 0)),
        place((few, n_rec, n_attr, thin), (0, 2, 1, 3)),
        place((few, n_attr, cols), (2, 1, 0)),
    ]))
    split = train_split[None, :]
    all_devices = n_rec * n_attr
    part = E // 2 // n_rec
    n_x = n_attr // 2

    def shape(*dims, dtype=BF16):
        return jax.ShapeDtypeStruct(dims, dtype)

    def vmem(*dims, dtype=BF16):
        return pltpu.VMEM(dims, dtype)

    args = (
        cells, cotangent, qkv_attr, out_attr, qkv_samp, out_samp, up_weight, down_weight.T, split, places
    )
    c_buf = vmem(n_attr, cols, few * E)
    g_buf = vmem(n_rec, thin * n_attr, few * E)
    f_buf = vmem(all_devices, thin, few * E)
    table = vmem(tokens, E)
    sums = []
    for count in COUNTS:
        h1 = count // 2
        h2 = h1 // n_x
        sums += [
            vmem(h1, n_rec, part, 2 * E), vmem(n_rec * n_x - 1, h2, part, 2 * E),
            vmem(h1, n_rec, part, 2 * E), pltpu.SemaphoreType.DMA((2, 2 * n_rec * n_x)),
        ]
    o_got, totals = pl.pallas_call(
        functools.partial(layer_kernel, width, size, length, few),
        out_shape=[shape(n_attr, cols, few * E), shape(BLOCKS, n_rec, part, 2 * E)],
        in_specs=[HBM] * len(args),
        out_specs=[HBM] * 2,
        scratch_shapes=[
            c_buf, vmem(BLOCKS, n_rec, part, 2 * E), pltpu.SemaphoreType.DMA((len(COUNTS) + 1,)),
        ]
        + [pltpu.VMEM(a.shape, a.dtype) for a in args]
        + [
            pltpu.SemaphoreType.DMA((len(args),)),
            vmem(tokens, E, dtype=F32), c_buf, c_buf, g_buf, g_buf, f_buf, f_buf, f_buf, f_buf, c_buf,
            table, vmem(E, tokens), vmem(3, E, tokens), vmem(tokens // width, HEADS, width, width, dtype=F32),
            table, table, vmem(3, E, tokens), vmem(tokens // size, HEADS, size, size, dtype=F32),
            vmem(3, E, tokens, dtype=F32), vmem(3, E, tokens), vmem(E, tokens), vmem(tokens, E, dtype=F32),
            vmem(tokens, E, dtype=F32), vmem(tokens, 1, dtype=F32), vmem(len(KEPT), tokens, tokens),
            vmem(2, 3, E, E), vmem(E, tokens), vmem(E, tokens),
            vmem(size, size, dtype=F32), vmem(BLOCKS, n_rec, part, 2 * E),
        ]
        + [
            pltpu.SemaphoreType.DMA((2, n))
            for n in (n_attr, n_rec, all_devices, all_devices, n_attr)
        ]
        + sums,
        compiler_params=pltpu.CompilerParams(
            collective_id=0, has_side_effects=True, vmem_limit_bytes=67043328
        ),
    )(*args)
    outs = [
        shape(rows, cols * E), shape(E, 3 * E, dtype=F32), shape(E, E, dtype=F32),
        shape(E, 3 * E, dtype=F32), shape(E, E, dtype=F32),
        shape(E, 4 * E, dtype=F32), shape(E, 4 * E, dtype=F32),
    ]
    last = (o_got, places, totals)
    out = pl.pallas_call(
        functools.partial(finish_kernel, 1.0 / math.sqrt(length * width), few),
        out_shape=outs,
        in_specs=[ANY] * 3,
        out_specs=[ANY] * len(outs),
        scratch_shapes=[pltpu.VMEM(a.shape, a.dtype) for a in (*last, *outs)]
        + [
            pltpu.SemaphoreType.DMA((6,)), pltpu.SemaphoreType.DMA((len(outs),)), vmem(tokens, E, dtype=F32), vmem(tokens, E, dtype=F32),
            vmem(BLOCKS, E // 2, 2 * E, dtype=F32),
        ],
        compiler_params=pltpu.CompilerParams(vmem_limit_bytes=67043328),
    )(*last)
    return (*out[:6], out[6].T)


def solution(mesh):
    both = P(("groups", "rec"), "attr")
    in_specs = (both, both, P(), P(), P(), P(), P(), P(), P("groups"))
    out_specs = (both,) + (P("groups", None),) * 6
    return jax.shard_map(local, mesh=mesh, in_specs=in_specs, out_specs=out_specs, check_vma=False)
```
